32 devices in a mesh: hyp: 2 (over y), row: 4 (over z), col: 4 (over x, core).
Axes of the slice: x: 2, y: 2, z: 4, core: 2. Of those that a mesh axis runs over, the one named last changes fastest.
Arguments:
- inverse_tile: float32 [16384, 8192], P(('hyp', 'row'), 'col'), parts along dimension 0, may hold values from -32768 to 262144, as said below
- panels: float32 [2, 2, 8192, 512], P('hyp', None, ('col', 'row')), parts along dimension 0, may hold values from -0.0007324219 to 0.0007324219
- link_panel: float32 [2, 512, 512], P('hyp'), parts along dimension 0, may hold values from -0.09375 to 0.09375
- diag_inverse: float32 [2, 2, 512, 512], P('hyp', None, 'row', 'col'), parts along dimension 0, may hold values from -3 to 3
- ancestor_tiles: int32 [1, 2, 64], replicated, may hold values 0 or 1
Outputs:
- ancestor_block: float32 [2, 2, 8192, 512], P('hyp', None, ('row', 'col')), parts along dimension 0
- diag_block: float32 [2, 2, 512, 512], P('hyp', None, 'row', 'col'), parts along dimension 0
- cross_block: float32 [2, 512, 512], P('hyp', 'row', 'col'), parts along dimension 0
The draws below stay inside these ranges and needn't reach their ends.
There are 2 independent parts, one for each index of `hyp`. The reference program is written for one: setup_inputs(seed, part) draws one part's arguments, and reference() takes and returns one part's arrays. A program takes and returns all parts, laid end to end along the dimension named above; an argument that names none is the same for every part. Nothing has to cross between parts.
Inputs may be any that keep to these rules, and one draw needn't show every extreme that they name: `inverse_tile`: symmetric.
All inputs are finite; a program needn't handle non-finite values.
Results may differ from the reference program's by a relative error of at most 0.000075.
Values sent between devices are 32-bit elements; how exact they have to be, the bound alone decides.
A program may use at most 128 MiB of HBM per device.

```python
import jax
import jax.numpy as jnp
from jax import lax

ANC = 8192
B = 512
TILE = 128
SIB = 1
TILES = 64


def draw_inverse_tile(key, part):
    noise_key = jax.random.fold_in(key, 11)
    diag_key = jax.random.fold_in(key, 23)
    noise = jax.random.normal(noise_key, (ANC, ANC), jnp.float32)
    spread = 0.35 * jnp.sqrt(jnp.float32(ANC))
    symmetric = (noise + noise.T) * spread
    diagonal = jax.random.uniform(diag_key, (ANC,), jnp.float32, 1.0, 2.0) * ANC
    matrix = symmetric + jnp.diag(diagonal - jnp.diagonal(symmetric))
    return matrix


def with_ends(values, rng, low, top_value):
    longest = values.shape.index(max(values.shape))
    spots = []
    for shift in (0, 1):
        where = [jax.random.randint(jax.random.fold_in(rng, axis), (), 0, length) for axis, length in enumerate(values.shape)]
        where[longest] = (where[longest] + shift) % values.shape[longest]
        spots.append(tuple(where))
    return values.at[spots[0]].set(low).at[spots[1]].set(top_value)


def shard_levels(stream_key, dims, split, smallest, top_value):
    level = 1.0
    for position, blocks in split:
        steps = jax.random.uniform(jax.random.fold_in(jax.random.fold_in(stream_key, 6), position), (blocks,), jnp.float32, smallest / len(split), top_value / len(split))
        level = level * jnp.repeat(jnp.exp(steps), dims[position] // blocks).reshape((-1,) + (1,) * (len(dims) - 1 - position))
    return level


def normal_values(key, shape, deviation, bound, shards=(), dtype=jnp.bfloat16):
    entries = jax.random.normal(key, shape, jnp.float32) * deviation
    if len(shards) > 0:
        entries = shard_levels(key, shape, shards, -0.22, 0.18) * entries
    return jnp.clip(entries, min=-bound, max=bound).astype(dtype)


def setup_inputs(seed: int = 0, part: int = 0) -> dict:
    seeds = jax.random.split(jax.random.key(seed), 6)
    own_keys = jax.random.split(jax.random.fold_in(seeds[5], part), 6)
    return {
        "inverse_tile": draw_inverse_tile(jax.random.fold_in(jax.random.fold_in(seeds[5], part), 71), part),
        "panels": normal_values(own_keys[1], (SIB, 2, ANC, B), (ANC * ANC) ** -0.5, 0.0007324219, ((2, 16),), jnp.float32),
        "link_panel": normal_values(own_keys[2], (SIB, B, B), (8 * B) ** -0.5, 0.09375, (), jnp.float32),
        "diag_inverse": normal_values(own_keys[3], (SIB, 2, B, B), 0.5, 3.0, ((2, 4), (3, 4)), jnp.float32),
        "ancestor_tiles": with_ends((jax.random.randint(seeds[4], (SIB, 2, TILES), 0, 4) < 3).astype(jnp.int32), jax.random.fold_in(seeds[4], 1), 0, 1),
    }


def reference(inverse_tile, panels, link_panel, diag_inverse, ancestor_tiles):
    precise = lax.Precision.HIGHEST
    rows_kept = jnp.repeat(ancestor_tiles, TILE, axis=2).astype(jnp.float32)
    masked = panels * rows_kept[..., None]
    first = masked[:, 0]
    second = masked[:, 1]
    ancestor_first = -jnp.einsum("ik,skb->sib", inverse_tile, first, precision=precise)
    diag_first = diag_inverse[:, 0] - jnp.einsum("sib,sic->sbc", first, ancestor_first, precision=precise)
    ancestor_second = -(jnp.einsum("ik,skb->sib", inverse_tile, second, precision=precise)
                        + jnp.einsum("sik,skc->sic", ancestor_first, link_panel, precision=precise))
    cross_block = -(jnp.einsum("sib,sic->sbc", ancestor_first, second, precision=precise)
                    + jnp.einsum("sbk,skc->sbc", diag_first, link_panel, precision=precise))
    diag_second = (diag_inverse[:, 1]
                   - jnp.einsum("sib,sic->sbc", second, ancestor_second, precision=precise)
                   - jnp.einsum("skb,skc->sbc", link_panel, cross_block, precision=precise))
    ancestor_block = jnp.stack([ancestor_first, ancestor_second], axis=1)
    diag_block = jnp.stack([diag_first, diag_second], axis=1)
    return ancestor_block, diag_block, cross_block
```

```python
import functools

import jax
import jax.numpy as jnp
from jax import lax
from jax.experimental import pallas as pl
from jax.experimental.pallas import tpu as pltpu
from jax.sharding import PartitionSpec as P

TILE = 128
MESH = pl.DeviceIdType.MESH


def mask_panels(panels, ancestor_tiles):
    rows_axis = lax.axis_size("row")
    local_rows = panels.shape[2]
    row_start = (lax.axis_index("col") * rows_axis + lax.axis_index("row")) * local_rows
    tile_mask = jnp.repeat(ancestor_tiles, TILE, axis=2)
    kept_rows = lax.dynamic_slice_in_dim(tile_mask, row_start, local_rows, 2)
    return jnp.where(kept_rows[..., None] != 0, panels, 0.0)


def exchange(axis_sizes, chunks, a_hbm, x_hbm, y_ref, own_ref, a_hi, a_lo, stage, p_hi, p_lo, gathered, partial,
             received, own, stage_sem, load_sem, send_sem, recv_sem, part_send, part_recv, own_send, own_recv, own_local):
    rows_axis, cols_axis = axis_sizes
    r = lax.axis_index("row")
    c = lax.axis_index("col")
    _, _, rows, width = gathered.shape
    half = rows // 2
    per_panel = chunks // x_hbm.shape[0]
    pieces = 2 * (rows_axis - 1)
    tile = stage.shape[1]
    tiles = a_hbm.shape[0] // tile

    def load(q):
        src = x_hbm.at[q // per_panel, :, pl.ds((q % per_panel) * width, width)]
        return pltpu.make_async_copy(src, gathered.at[q, r], load_sem.at[q])

    def stage_copy(i):
        src = a_hbm.at[pl.ds(pl.multiple_of(i * tile, tile), tile)]
        return pltpu.make_async_copy(src, stage.at[i % 2], stage_sem.at[i % 2])

    def hop(q, block, h, way, target):
        ref = gathered.at[q, block, pl.ds(pl.multiple_of(h * half, half), half)]
        return pltpu.make_async_remote_copy(
            ref, ref, send_sem.at[way, q, block, h], recv_sem.at[q, block, h],
            device_id={"row": target}, device_id_type=MESH)

    def each_send(q, s, h, act):
        @pl.when((r + 1 < rows_axis) & (r - s >= 0))
        def _():
            act(hop(q, r - s, h, 0, r + 1))

        @pl.when((r >= 1) & (r + s < rows_axis))
        def _():
            act(hop(q, r + s, h, 1, r - 1))

    def wait_arrivals(q, s, h):
        @pl.when(r - 1 - s >= 0)
        def _():
            hop(q, r - 1 - s, h, 0, r - 1).wait_recv()

            @pl.when(h == 1)
            def _():
                own_of_block(q, r - 1 - s)

        @pl.when(r + 1 + s < rows_axis)
        def _():
            hop(q, r + 1 + s, h, 1, r + 1).wait_recv()

            @pl.when(h == 1)
            def _():
                own_of_block(q, r + 1 + s)

    def part(q, target, source):
        return pltpu.make_async_remote_copy(
            partial.at[q, target], received.at[q, source], part_send.at[q, target], part_recv.at[q, source],
            device_id={"col": target}, device_id_type=MESH)

    def own_copy(q, target):
        return pltpu.make_async_remote_copy(
            gathered.at[q, (r * cols_axis + target) % rows_axis], own.at[q], own_send.at[q, target], own_recv.at[q],
            device_id={"col": target}, device_id_type=MESH)

    def own_here(q):
        return pltpu.make_async_copy(gathered.at[q, (r * cols_axis + c) % rows_axis], own.at[q], own_local.at[q])

    own_root = (r * cols_axis + c) // rows_axis

    def own_of_block(q, block):
        for shift in range(1, cols_axis):
            target = (c + shift) % cols_axis
            place = r * cols_axis + target

            @pl.when((place // rows_axis == c) & (place % rows_axis == block))
            def _():
                own_copy(q, target).start()

    def each_own(q, act):
        for shift in range(1, cols_axis):
            target = (c + shift) % cols_axis

            @pl.when((r * cols_axis + target) // rows_axis == c)
            def _():
                act(own_copy(q, target))

    for q in range(chunks):
        load(q).start()
    stage_copy(0).start()
    barrier = pltpu.get_barrier_semaphore()
    for shift in range(1, cols_axis):
        pl.semaphore_signal(barrier, inc=1, device_id={"col": (c + shift) % cols_axis}, device_id_type=MESH)

    @pl.when(r >= 1)
    def _():
        pl.semaphore_signal(barrier, inc=1, device_id={"row": r - 1}, device_id_type=MESH)

    @pl.when(r + 1 < rows_axis)
    def _():
        pl.semaphore_signal(barrier, inc=1, device_id={"row": r + 1}, device_id_type=MESH)

    inner = (r >= 1) & (r + 1 < rows_axis)

    @pl.when(inner)
    def _():
        pl.semaphore_wait(barrier, cols_axis + 1)

    @pl.when(jnp.logical_not(inner))
    def _():
        pl.semaphore_wait(barrier, cols_axis)

    for q in range(chunks):
        load(q).wait()

    def split_tile(i, carry):
        @pl.when(i + 1 < tiles)
        def _():
            stage_copy(i + 1).start()

        stage_copy(i).wait()
        at = pl.ds(pl.multiple_of(i * tile, tile), tile)
        value = stage[i % 2]
        high = value.astype(jnp.bfloat16)
        a_hi[at, :] = high
        a_lo[at, :] = (value - high.astype(jnp.float32)).astype(jnp.bfloat16)
        return carry

    def multiply(k, i):
        even = 1 - 2 * (c % 2)
        target = (c + cols_axis // 2 + even * i + cols_axis) % cols_axis
        at = pl.ds(pl.multiple_of(target * rows, rows), rows)
        high = a_hi[at, :]
        out = jnp.dot(high, p_hi[...], preferred_element_type=jnp.float32)
        out += jnp.dot(high, p_lo[...], preferred_element_type=jnp.float32)
        out += jnp.dot(a_lo[at, :], p_hi[...], preferred_element_type=jnp.float32)
        partial[k, target] = out

        @pl.when(target != c)
        def _():
            part(k, target, c).start()

    def step(u, carry):
        q, p = u // pieces, u % pieces
        s, h = p // 2, p % 2

        @pl.when((u >= 2) & (u < chunks * pieces + 2))
        def _():
            v = u - 2
            wait_arrivals(v // pieces, (v % pieces) // 2, v % 2)

        @pl.when(q < chunks)
        def _():
            each_send(q, s, h, lambda copy: copy.start())

        @pl.when((q < chunks) & (p == 0))
        def _():
            own_of_block(q, r)

        @pl.when(u == 1)
        def _():
            lax.fori_loop(0, tiles, split_tile, 0)

        @pl.when((q >= 1) & (p == 1))
        def _():
            k = q - 1

            @pl.when(own_root == c)
            def _():
                own_here(k).start()

            def split_panel(b, carry):
                at = pl.ds(pl.multiple_of(b * rows, rows), rows)
                value = gathered[k, b]
                high = value.astype(jnp.bfloat16)
                p_hi[at, :] = high
                p_lo[at, :] = (value - high.astype(jnp.float32)).astype(jnp.bfloat16)
                return carry

            lax.fori_loop(0, rows_axis, split_panel, 0)

        @pl.when((q >= 1) & (p >= 1))
        def _():
            def body(i, carry):
                multiply(q - 1, i)
                return carry

            lax.fori_loop((p - 1) * cols_axis // (pieces - 1), p * cols_axis // (pieces - 1), body, 0)

        return carry

    lax.fori_loop(0, (chunks + 1) * pieces, step, 0)

    for q in range(chunks):
        panel, start = q // per_panel, (q % per_panel) * width
        at = (panel, slice(None), slice(start, start + width))
        total = partial[q, c]
        for shift in range(1, cols_axis):
            source = (c + shift) % cols_axis
            part(q, source, source).wait_recv()
            total += received[q, source]
        y_ref[at] = total

        @pl.when(own_root == c)
        def _():
            own_here(q).wait()

        @pl.when(own_root != c)
        def _():
            own_copy(q, own_root).wait_recv()

        own_ref[at] = own[q]

    def drain(u, carry):
        q, p = u // pieces, u % pieces
        each_send(q, p // 2, p % 2, lambda copy: copy.wait_send())
        return carry

    lax.fori_loop(0, chunks * pieces, drain, 0)
    for q in range(chunks):
        each_own(q, lambda copy: copy.wait_send())
        for shift in range(1, cols_axis):
            part(q, (c + shift) % cols_axis, c).wait_send()


def products(inverse_tile, masked):
    rows_axis, cols_axis = lax.axis_size("row"), lax.axis_size("col")
    height, depth = inverse_tile.shape
    count, rows, columns = masked.shape
    width = min(256, columns)
    chunks = count * columns // width
    tile = min(128, height)
    f32, bf16 = jnp.float32, jnp.bfloat16
    dma = pltpu.SemaphoreType.DMA
    result = jax.ShapeDtypeStruct((count, rows, columns), f32)
    return pl.pallas_call(
        functools.partial(exchange, (rows_axis, cols_axis), chunks),
        out_shape=(result, result),
        in_specs=[pl.BlockSpec(memory_space=pl.ANY)] * 2,
        out_specs=[pl.BlockSpec(memory_space=pltpu.VMEM)] * 2,
        scratch_shapes=[
            pltpu.VMEM((height, depth), bf16),
            pltpu.VMEM((height, depth), bf16),
            pltpu.VMEM((2, tile, depth), f32),
            pltpu.VMEM((depth, width), bf16),
            pltpu.VMEM((depth, width), bf16),
            pltpu.VMEM((chunks, rows_axis, rows, width), f32),
            pltpu.VMEM((chunks, cols_axis, rows, width), f32),
            pltpu.VMEM((chunks, cols_axis, rows, width), f32),
            pltpu.VMEM((chunks, rows, width), f32),
            dma((2,)),
            dma((chunks,)),
            dma((2, chunks, rows_axis, 2)),
            dma((chunks, rows_axis, 2)),
            dma((chunks, cols_axis)),
            dma((chunks, cols_axis)),
            dma((chunks, cols_axis)),
            dma((chunks,)),
            dma((chunks,)),
        ],
        compiler_params=pltpu.CompilerParams(
            collective_id=0, has_side_effects=True, vmem_limit_bytes=60 * 1024 * 1024),
    )(inverse_tile, masked)


def halving_levels():
    levels = []
    for axis in ("col", "row"):
        dist = 1
        while dist < lax.axis_size(axis):
            levels.append((axis, dist))
            dist *= 2
    return levels


def split(value):
    high = value.astype(jnp.bfloat16)
    return high, (value - high.astype(jnp.float32)).astype(jnp.bfloat16)


def dot3(a, b, contract):
    def one(left, right):
        return lax.dot_general(
            left, right, (((contract,), (0,)), ((), ())), preferred_element_type=jnp.float32)

    return one(a[0], b[0]) + (one(a[0], b[1]) + one(a[1], b[0]))


def finish_kernel(levels, count, y_ref, own_ref, link_ref, given_ref, anc_ref, diag_ref, cross_ref, terms, out_ref, *scratch):
    depth = len(levels)
    height, span = given_ref.shape[1:]
    rows_axis, cols_axis = terms.shape[3], 2 * terms.shape[1]
    kept = (terms,) + scratch[: depth - 1]
    landed = scratch[depth - 1 : 2 * depth - 1]
    send_sem, recv_sem = scratch[2 * depth - 1 :]

    def bit_and_partner(level):
        axis, dist = levels[level]
        at = lax.axis_index(axis)
        bit = (at // dist) % 2
        return bit, {axis: at + dist * (1 - 2 * bit)}

    def copy(level, k):
        bit, partner = bit_and_partner(level)
        return pltpu.make_async_remote_copy(
            kept[level].at[k, :, 1 - bit], landed[level].at[k], send_sem.at[level, k], recv_sem.at[level, k],
            device_id=partner, device_id_type=MESH)

    barrier = pltpu.get_barrier_semaphore()
    for level in range(depth):
        pl.semaphore_signal(barrier, inc=1, device_id=bit_and_partner(level)[1], device_id_type=MESH)
    pl.semaphore_wait(barrier, depth)

    def store(k, value):
        for col in range(cols_axis):
            for row in range(rows_axis):
                terms[k, col // 2, col % 2, row] = value[
                    row * height : (row + 1) * height, col * span : (col + 1) * span]

    row_id, col_id = lax.axis_index("row"), lax.axis_index("col")
    y1 = -y_ref[0]
    anc_ref[0] = y1
    first, y1_parts = split(own_ref[0]), split(y1)
    store(0, dot3(first, y1_parts, 0))
    copy(0, 0).start()
    link = split(link_ref[...])
    link_cols = link_ref[pl.ds(pl.multiple_of(col_id * span, span), span), :]
    link_rows = link_ref[pl.ds(pl.multiple_of(row_id * height, height), height), :]
    given = dot3(split(given_ref[0]), split(link_cols), 1)
    y2 = -(y_ref[1] + dot3(y1_parts, link, 1))
    anc_ref[1] = y2
    y2_parts = split(y2)
    store(1, dot3(first, y2_parts, 0))
    for col in range(cols_axis):
        terms[1, col // 2, col % 2, row_id] += given[:, col * span : (col + 1) * span]
    copy(0, 1).start()
    shifted = split(own_ref[1] - dot3(first, link, 1))
    store(2, dot3(shifted, y2_parts, 0) - dot3(split(link_rows), split(given), 0))
    copy(0, 2).start()

    for level in range(1, depth + 1):
        for k in range(count):
            copy(level - 1, k).wait_recv()
            bit, _ = bit_and_partner(level - 1)
            total = kept[level - 1][k, :, bit] + landed[level - 1][k]
            target = kept[level] if level < depth else out_ref
            target[k] = total.reshape(target.shape[1:])
            if level < depth:
                copy(level, k).start()
    diag_ref[0] = given_ref[0] - out_ref[0]
    diag_ref[1] = given_ref[1] - out_ref[2]
    cross_ref[...] = -out_ref[1]
    for level in range(depth):
        for k in range(count):
            copy(level, k).wait_send()


def finish(y, own, link, given):
    rows_axis, cols_axis = lax.axis_size("row"), lax.axis_size("col")
    count = 3
    height, span = given.shape[1:]
    levels = halving_levels()
    shapes = []
    cols, rows = cols_axis, rows_axis
    for axis, _ in levels:
        if axis == "col":
            cols //= 2
            shapes.append(((cols, 2, rows, height, span), (cols, rows, height, span)))
        else:
            rows //= 2
            shapes.append(((rows, 2, height, span), (rows, height, span)))
    dma = pltpu.SemaphoreType.DMA((len(levels), count))
    return pl.pallas_call(
        functools.partial(finish_kernel, levels, count),
        out_shape=(
            jax.ShapeDtypeStruct(y.shape, jnp.float32),
            jax.ShapeDtypeStruct(given.shape, jnp.float32),
            jax.ShapeDtypeStruct((height, span), jnp.float32),
        ),
        in_specs=[pl.BlockSpec(memory_space=pltpu.VMEM)] * 4,
        out_specs=[pl.BlockSpec(memory_space=pltpu.VMEM)] * 3,
        scratch_shapes=[
            pltpu.VMEM((count,) + shapes[0][0], jnp.float32),
            pltpu.VMEM((count, height, span), jnp.float32),
        ]
        + [pltpu.VMEM((count,) + kept, jnp.float32) for kept, _ in shapes[1:]]
        + [pltpu.VMEM((count,) + landed, jnp.float32) for _, landed in shapes]
        + [dma, dma],
        compiler_params=pltpu.CompilerParams(
            collective_id=1, has_side_effects=True, vmem_limit_bytes=48 * 1024 * 1024),
    )(y, own, link, given)


def order_of(r, count, i):
    near = jnp.minimum(r, count - 1 - r)
    close = r + ((i + 1) // 2) * (1 - 2 * (i % 2))
    far = jnp.where(2 * r < count - 1, r + i - near, r - i + near)
    return jnp.where(i <= 2 * near, close, far)


def fused_kernel(axis_sizes, tiles_ref, a_hbm, x_hbm, link_hbm, given_hbm, anc_ref, diag_ref, cross_ref,
                 a_hi, a_lo, stage, pieces, gathered, partial, pair_in, group_in, own, link, given, shift_x, shift_y,
                 given_link, term, term_pair, term_group, term_row,
                 stage_sem, load_sem, small_sem, hop_send, hop_recv, pair_send, pair_recv, group_send, group_recv,
                 own_send, own_recv, tp_send, tp_recv, tg_send, tg_recv, tr_send, tr_recv):
    rows_axis, cols_axis = axis_sizes
    groups = cols_axis // 2
    r = lax.axis_index("row")
    c = lax.axis_index("col")
    g, k = c // 2, c % 2
    chunks, _, rows, width = gathered.shape
    height, span = given.shape[1:]
    tile = stage.shape[1]
    tiles = a_hbm.shape[0] // tile
    last = chunks - 1

    def remote(src, dst, send, recv, **where):
        return pltpu.make_async_remote_copy(src, dst, send, recv, device_id=where, device_id_type=MESH)

    def load(q):
        src = x_hbm.at[q // cols_axis, :, pl.ds(pl.multiple_of((q % cols_axis) * width, width), width)]
        return pltpu.make_async_copy(src, gathered.at[q, r], load_sem.at[q])

    def stage_copy(i):
        src = a_hbm.at[pl.ds(pl.multiple_of(i * tile, tile), tile)]
        return pltpu.make_async_copy(src, stage.at[i % 2], stage_sem.at[i % 2])

    def hop(q, block, way, target):
        ref = gathered.at[q, block]
        return remote(ref, ref, hop_send.at[way, q, block], hop_recv.at[q, block], row=target)

    def send_own_block(q):
        @pl.when(r + 1 < rows_axis)
        def _():
            hop(q, r, 0, r + 1).start()

        @pl.when(r >= 1)
        def _():
            hop(q, r, 1, r - 1).start()

    def pair_copy(q, t):
        return remote(partial.at[q, 2 * t + 1 - k], pair_in.at[q, t], pair_send.at[q, t], pair_recv.at[q, t],
                      col=c + 1 - 2 * k)

    def group_copy(q, shift):
        target = 2 * ((g + shift) % groups) + k
        return remote(partial.at[q, target], group_in.at[q, shift - 1], group_send.at[q, shift - 1],
                      group_recv.at[q, shift - 1], col=target)

    def own_copy(q, target):
        return remote(gathered.at[q, (r * cols_axis + target) % rows_axis], own.at[q], own_send.at[q, target],
                      own_recv.at[q], col=target)

    own_root = (r * cols_axis + c) // rows_axis

    def each_own(act, block=None):
        for shift in range(1, cols_axis):
            target = (c + shift) % cols_axis
            place = r * cols_axis + target
            mine = place // rows_axis == c
            if block is not None:
                mine = mine & (place % rows_axis == block)

            @pl.when(mine)
            def _():
                act(target)

    def own_ready(q):
        @pl.when(own_root == c)
        def _():
            own[q] = gathered[q, (r * cols_axis + c) % rows_axis]

        @pl.when(own_root != c)
        def _():
            own_copy(q, c).wait_recv()

    def tp_copy(n, j):
        return remote(term.at[n, j], term_pair.at[n, j // 2], tp_send.at[n, j], tp_recv.at[n, j],
                      col=c + 1 - 2 * k)

    def tg_copy(n, j, shift):
        return remote(term.at[n, j], term_group.at[n, shift - 1], tg_send.at[n, j],
                      tg_recv.at[n, shift - 1], col=j)

    def tr_copy(n, target):
        return remote(term.at[n, c, target], term_row.at[n, r], tr_send.at[n, target],
                      tr_recv.at[n, r], row=target)

    def tr_wait(n, source):
        return remote(term.at[n, c, source], term_row.at[n, source], tr_send.at[n, source],
                      tr_recv.at[n, source], row=source)

    def term_start(n, j):
        @pl.when(j % 2 != k)
        def _():
            tp_copy(n, j).start()

    def term_mid(n, j):
        @pl.when(j % 2 == k)
        def _():
            tp_copy(n, j).wait_recv()
            term[n, j] += term_pair[n, j // 2]

            @pl.when(j != c)
            def _():
                tg_copy(n, j, (j // 2 - g + groups) % groups).start()

    def term_far(n, j):
        @pl.when(j == c)
        def _():
            total = term[n, j]
            for shift in range(1, groups):
                tg_copy(n, j, shift).wait_recv()
                total += term_group[n, shift - 1]
            term[n, j] = total
            for shift in range(1, rows_axis):
                tr_copy(n, (r + shift) % rows_axis).start()

    def term_end(n):
        total = term[n, c, r]
        for shift in range(1, rows_axis):
            source = (r + shift) % rows_axis
            tr_wait(n, source).wait_recv()
            total += term_row[n, source]
        return total

    def term_drain(n, j):
        @pl.when(j % 2 != k)
        def _():
            tp_copy(n, j).wait_send()

        @pl.when((j % 2 == k) & (j != c))
        def _():
            tg_copy(n, j, (j // 2 - g + groups) % groups).wait_send()

    def each_column(act, stop=cols_axis):
        def body(j, carry):
            act(j)
            return carry

        lax.fori_loop(0, stop, body, 0)

    def wide(ref, start, stop):
        return jnp.concatenate([ref[start + j] for j in range(stop)], axis=1)

    for q in range(chunks):
        load(q).start()
    small = [pltpu.make_async_copy(link_hbm, link, small_sem.at[0]),
             pltpu.make_async_copy(given_hbm, given, small_sem.at[1])]
    stage_copy(0).start()
    stage_copy(1).start()
    for copy in small:
        copy.start()
    barrier = pltpu.get_barrier_semaphore()
    for shift in range(1, cols_axis):
        pl.semaphore_signal(barrier, inc=1, device_id={"col": (c + shift) % cols_axis}, device_id_type=MESH)
    for shift in range(1, rows_axis):
        pl.semaphore_signal(barrier, inc=1, device_id={"row": (r + shift) % rows_axis}, device_id_type=MESH)

    per_block = rows // TILE
    first_tile = (c * rows_axis + r) * per_block

    def mask(q, carry):
        load(q).wait()
        for s in range(per_block):
            kept = (tiles_ref[q // cols_axis, first_tile + s] != 0).astype(jnp.float32)
            at = pl.ds(s * TILE, TILE)
            gathered[q, r, at] = gathered[q, r, at] * kept
        return carry

    lax.fori_loop(0, 2, mask, 0)
    pl.semaphore_wait(barrier, cols_axis + rows_axis - 2)
    send_own_block(0)
    send_own_block(1)
    lax.fori_loop(2, chunks, mask, 0)

    def split_tile(i, carry):
        stage_copy(i).wait()
        at = pl.ds(pl.multiple_of(i * tile, tile), tile)
        value = stage[i % 2]
        high = value.astype(jnp.bfloat16)
        a_hi[at, :] = high
        a_lo[at, :] = (value - high.astype(jnp.float32)).astype(jnp.bfloat16)

        @pl.when(i + 2 < tiles)
        def _():
            stage_copy(i + 2).start()

        return carry

    lax.fori_loop(0, tiles, split_tile, 0)

    def multiply(q, block, first):
        value = gathered[q, block]
        high = value.astype(jnp.bfloat16)
        pieces[:, :width] = high
        pieces[:, width:] = (value - high.astype(jnp.float32)).astype(jnp.bfloat16)
        inner = pl.ds(pl.multiple_of(block * rows, rows), rows)

        def body(i, carry):
            t = (c + 1 + i) % cols_axis
            at = pl.ds(pl.multiple_of(t * rows, rows), rows)
            both = jnp.dot(a_hi[at, inner], pieces[...], preferred_element_type=jnp.float32)
            out = jnp.dot(a_lo[at, inner], pieces[:, :width], preferred_element_type=jnp.float32)
            out += both[:, width:]
            out += both[:, :width]
            if first:
                partial[q, t] = out
            else:
                partial[q, t] += out
            return carry

        lax.fori_loop(0, cols_axis, body, 0)

    def pair_start(q):
        for t in range(groups):
            pair_copy(q, t).start()

    def pair_finish(q):
        for t in range(groups):
            pair_copy(q, t).wait_recv()
        for shift in range(1, groups):
            far = (g + shift) % groups
            partial[q, 2 * far + k] += pair_in[q, far]
            group_copy(q, shift).start()

    def total_of(q):
        total = partial[q, c] + pair_in[q, g]
        for shift in range(1, groups):
            group_copy(q, shift).wait_recv()
            total += group_in[q, shift - 1]
        return total

    def store_terms(n, value, j):
        for i in range(rows_axis):
            term[n, j, i] = value[i * height : (i + 1) * height]

    def first_done(_):
        for j in range(cols_axis):
            own_ready(j)
        y_parts = split(-anc_ref[0])
        x_parts = split(wide(own, 0, cols_axis))
        value = dot3(x_parts, y_parts, 0)
        for j in range(cols_axis):
            store_terms(0, value[:, j * span : (j + 1) * span], j)
        each_column(lambda j: term_start(0, j))
        for copy in small:
            copy.wait()
        link_parts = split(link[...])
        value = dot3(y_parts, link_parts, 1)
        for j in range(cols_axis):
            shift_y[j] = value[:, j * width : (j + 1) * width]
        value = dot3(x_parts, link_parts, 1)
        for j in range(cols_axis):
            shift_x[j] = value[:, j * width : (j + 1) * width]
        link_cols = link[pl.ds(pl.multiple_of(c * span, span), span), :]
        value = dot3(split(given[0]), split(link_cols), 1)
        for j in range(cols_axis):
            given_link[j] = value[:, j * span : (j + 1) * span]

    def own_shifted(j):
        own_ready(cols_axis + j)
        own[cols_axis + j] -= shift_x[j]

    def cross_term(j):
        value = dot3(split(anc_ref[0]), split(own[cols_axis + j]), 0)
        store_terms(1, -value, j)
        term[1, j, r] -= given_link[j]
        term_start(1, j)

    def second_chunk(j, total):
        value = shift_y[j] - total
        anc_ref[1, :, pl.ds(pl.multiple_of(j * width, width), width)] = value

    def chunk(q, carry):
        prior = q - 1

        @pl.when((q >= 1) & (q < last))
        def _():
            send_own_block(q + 1)

        each_own(lambda target: own_copy(q, target).start(), r)
        multiply(q, r, True)
        for i in range(1, rows_axis):
            block = order_of(r, rows_axis, i)
            wait_and_forward(q, block)
            each_own(lambda target: own_copy(q, target).start(), block)
            multiply(q, block, False)
            if i == 1:
                @pl.when(q >= 1)
                def _():
                    pair_finish(prior)

                @pl.when(q == cols_axis + 1)
                def _():
                    each_column(lambda j: term_mid(0, j))

                @pl.when(q >= cols_axis + 2)
                def _():
                    term_mid(1, q - cols_axis - 2)

            if i == rows_axis - 1:
                @pl.when((q >= 1) & (q <= cols_axis))
                def _():
                    at = pl.ds(pl.multiple_of(prior * width, width), width)
                    anc_ref[0, :, at] = -total_of(prior)

                @pl.when(q == cols_axis)
                def _():
                    first_done(None)

                @pl.when(q == cols_axis + 1)
                def _():
                    each_column(lambda j: term_far(0, j))

                @pl.when(q >= cols_axis + 2)
                def _():
                    term_far(1, q - cols_axis - 2)

                @pl.when(q >= cols_axis + 1)
                def _():
                    j = prior - cols_axis
                    second_chunk(j, total_of(prior))
                    own_shifted(j)
                    cross_term(j)

        pair_start(q)
        return carry

    def wait_and_forward(q, block):
        @pl.when(block < r)
        def _():
            hop(q, block, 0, r - 1).wait_recv()

            @pl.when(r + 1 < rows_axis)
            def _():
                hop(q, block, 0, r + 1).start()

        @pl.when(block > r)
        def _():
            hop(q, block, 1, r + 1).wait_recv()

            @pl.when(r >= 1)
            def _():
                hop(q, block, 1, r - 1).start()

    lax.fori_loop(0, chunks, chunk, 0)

    end = cols_axis - 1
    pair_finish(last)
    own_shifted(end)
    cross_term(end)
    term_mid(1, end - 1)
    link_rows = link[pl.ds(pl.multiple_of(r * height, height), height), :]
    base = dot3(split(link_rows), split(jnp.concatenate([given_link[j] for j in range(cols_axis)], axis=1)), 0)
    shifted = split(wide(own, cols_axis, cols_axis))
    for j in range(cols_axis - 1):
        value = base[:, j * span : (j + 1) * span] - dot3(
            shifted, split(anc_ref[1, :, j * width : (j + 1) * width]), 0)
        store_terms(2, value, j)
        term_start(2, j)
    term_far(1, end - 1)
    second_chunk(end, total_of(last))
    value = base[:, end * span :] - dot3(shifted, split(anc_ref[1, :, end * width :]), 0)
    store_terms(2, value, end)
    term_start(2, end)
    each_column(lambda j: term_mid(2, j))
    term_mid(1, end)
    each_column(lambda j: term_far(2, j))
    term_far(1, end)
    diag_ref[0] = given[0] + term_end(0)
    cross_ref[...] = term_end(1)
    diag_ref[1] = given[1] + term_end(2)

    def drain(q, carry):
        def body(block, carry):
            @pl.when((block <= r) & (r + 1 < rows_axis))
            def _():
                hop(q, block, 0, r + 1).wait_send()

            @pl.when((block >= r) & (r >= 1))
            def _():
                hop(q, block, 1, r - 1).wait_send()

            return carry

        lax.fori_loop(0, rows_axis, body, 0)
        each_own(lambda target: own_copy(q, target).wait_send())
        for t in range(groups):
            pair_copy(q, t).wait_send()
        for shift in range(1, groups):
            group_copy(q, shift).wait_send()
        return carry

    lax.fori_loop(0, chunks, drain, 0)
    for n in range(3):
        each_column(lambda j: term_drain(n, j))
        for shift in range(1, rows_axis):
            tr_copy(n, (r + shift) % rows_axis).wait_send()


def fused(inverse_tile, panels, link_panel, given, tiles):
    rows_axis, cols_axis = lax.axis_size("row"), lax.axis_size("col")
    groups = cols_axis // 2
    full, depth = inverse_tile.shape
    count, rows, columns = panels.shape
    height, span = given.shape[1:]
    width = span
    chunks = count * cols_axis
    tile = min(128, full)
    f32, bf16 = jnp.float32, jnp.bfloat16
    dma = pltpu.SemaphoreType.DMA
    vmem = pltpu.VMEM
    return pl.pallas_call(
        functools.partial(fused_kernel, (rows_axis, cols_axis)),
        out_shape=(
            jax.ShapeDtypeStruct((count, rows, columns), f32),
            jax.ShapeDtypeStruct(given.shape, f32),
            jax.ShapeDtypeStruct((height, span), f32),
        ),
        in_specs=[pl.BlockSpec(memory_space=pltpu.SMEM)] + [pl.BlockSpec(memory_space=pl.ANY)] * 4,
        out_specs=[pl.BlockSpec(memory_space=vmem)] * 3,
        scratch_shapes=[
            vmem((full, depth), bf16),
            vmem((full, depth), bf16),
            vmem((2, tile, depth), f32),
            vmem((rows, 2 * width), bf16),
            vmem((chunks, rows_axis, rows, width), f32),
            vmem((chunks, cols_axis, rows, width), f32),
            vmem((chunks, groups, rows, width), f32),
            vmem((chunks, max(groups - 1, 1), rows, width), f32),
            vmem((chunks, rows, width), f32),
            vmem((columns, columns), f32),
            vmem(given.shape, f32),
            vmem((cols_axis, rows, width), f32),
            vmem((cols_axis, rows, width), f32),
            vmem((cols_axis, height, span), f32),
            vmem((3, cols_axis, rows_axis, height, span), f32),
            vmem((3, groups, rows_axis, height, span), f32),
            vmem((3, max(groups - 1, 1), rows_axis, height, span), f32),
            vmem((3, rows_axis, height, span), f32),
            dma((2,)),
            dma((chunks,)),
            dma((2,)),
            dma((2, chunks, rows_axis)),
            dma((chunks, rows_axis)),
            dma((chunks, groups)),
            dma((chunks, groups)),
            dma((chunks, max(groups - 1, 1))),
            dma((chunks, max(groups - 1, 1))),
            dma((chunks, cols_axis)),
            dma((chunks,)),
            dma((3, cols_axis)),
            dma((3, cols_axis)),
            dma((3, cols_axis)),
            dma((3, max(groups - 1, 1))),
            dma((3, rows_axis)),
            dma((3, rows_axis)),
        ],
        compiler_params=pltpu.CompilerParams(
            collective_id=2, has_side_effects=True, vmem_limit_bytes=62 * 1024 * 1024),
    )(tiles, inverse_tile, panels, link_panel, given)


def local(inverse_tile, panels, link_panel, diag_inverse, ancestor_tiles):
    rows_axis, cols_axis = lax.axis_size("row"), lax.axis_size("col")
    rows, columns = panels.shape[2:]
    square = rows % TILE == 0 and (columns // cols_axis) % 128 == 0 and cols_axis % 2 == 0 and rows_axis > 1
    if square:
        anc, diag, cross = fused(inverse_tile, panels[0], link_panel[0], diag_inverse[0], ancestor_tiles[0])
    else:
        masked = mask_panels(panels, ancestor_tiles)[0]
        ys, own = products(inverse_tile, masked)
        anc, diag, cross = finish(ys, own, link_panel[0], diag_inverse[0])
    return anc[None], diag[None], cross[None]


def solution(mesh):
    in_specs = (
        P(("hyp", "row"), "col"),
        P("hyp", None, ("col", "row"), None),
        P("hyp", None, None),
        P("hyp", None, "row", "col"),
        P(),
    )
    out_specs = (
        P("hyp", None, ("row", "col"), None),
        P("hyp", None, "row", "col"),
        P("hyp", "row", "col"),
    )
    return jax.shard_map(local, mesh=mesh, in_specs=in_specs, out_specs=out_specs, check_vma=False)
```

```python
import functools

import jax
import jax.numpy as jnp
from jax import lax
from jax.experimental import pallas as pl
from jax.experimental.pallas import tpu as pltpu
from jax.sharding import PartitionSpec as P

TILE = 128
MESH = pl.DeviceIdType.MESH


def mask_panels(panels, ancestor_tiles):
    rows_axis = lax.axis_size("row")
    local_rows = panels.shape[2]
    row_start = (lax.axis_index("col") * rows_axis + lax.axis_index("row")) * local_rows
    tile_mask = jnp.repeat(ancestor_tiles, TILE, axis=2)
    kept_rows = lax.dynamic_slice_in_dim(tile_mask, row_start, local_rows, 2)
    return jnp.where(kept_rows[..., None] != 0, panels, 0.0)


def exchange(axis_sizes, chunks, a_hbm, x_hbm, y_ref, own_ref, a_hi, a_lo, stage, p_hi, p_lo, gathered, partial,
             received, own, stage_sem, load_sem, send_sem, recv_sem, part_send, part_recv, own_send, own_recv, own_local):
    rows_axis, cols_axis = axis_sizes
    r = lax.axis_index("row")
    c = lax.axis_index("col")
    _, _, rows, width = gathered.shape
    half = rows // 2
    per_panel = chunks // x_hbm.shape[0]
    pieces = 2 * (rows_axis - 1)
    tile = stage.shape[1]
    tiles = a_hbm.shape[0] // tile

    def load(q):
        src = x_hbm.at[q // per_panel, :, pl.ds((q % per_panel) * width, width)]
        return pltpu.make_async_copy(src, gathered.at[q, r], load_sem.at[q])

    def stage_copy(i):
        src = a_hbm.at[pl.ds(pl.multiple_of(i * tile, tile), tile)]
        return pltpu.make_async_copy(src, stage.at[i % 2], stage_sem.at[i % 2])

    def hop(q, block, h, way, target):
        ref = gathered.at[q, block, pl.ds(pl.multiple_of(h * half, half), half)]
        return pltpu.make_async_remote_copy(
            ref, ref, send_sem.at[way, q, block, h], recv_sem.at[q, block, h],
            device_id={"row": target}, device_id_type=MESH)

    def each_send(q, s, h, act):
        @pl.when((r + 1 < rows_axis) & (r - s >= 0))
        def _():
            act(hop(q, r - s, h, 0, r + 1))

        @pl.when((r >= 1) & (r + s < rows_axis))
        def _():
            act(hop(q, r + s, h, 1, r - 1))

    def wait_arrivals(q, s, h):
        @pl.when(r - 1 - s >= 0)
        def _():
            hop(q, r - 1 - s, h, 0, r - 1).wait_recv()

            @pl.when(h == 1)
            def _():
                own_of_block(q, r - 1 - s)

        @pl.when(r + 1 + s < rows_axis)
        def _():
            hop(q, r + 1 + s, h, 1, r + 1).wait_recv()

            @pl.when(h == 1)
            def _():
                own_of_block(q, r + 1 + s)

    def part(q, target, source):
        return pltpu.make_async_remote_copy(
            partial.at[q, target], received.at[q, source], part_send.at[q, target], part_recv.at[q, source],
            device_id={"col": target}, device_id_type=MESH)

    def own_copy(q, target):
        return pltpu.make_async_remote_copy(
            gathered.at[q, (r * cols_axis + target) % rows_axis], own.at[q], own_send.at[q, target], own_recv.at[q],
            device_id={"col": target}, device_id_type=MESH)

    def own_here(q):
        return pltpu.make_async_copy(gathered.at[q, (r * cols_axis + c) % rows_axis], own.at[q], own_local.at[q])

    own_root = (r * cols_axis + c) // rows_axis

    def own_of_block(q, block):
        for shift in range(1, cols_axis):
            target = (c + shift) % cols_axis
            place = r * cols_axis + target

            @pl.when((place // rows_axis == c) & (place % rows_axis == block))
            def _():
                own_copy(q, target).start()

    def each_own(q, act):
        for shift in range(1, cols_axis):
            target = (c + shift) % cols_axis

            @pl.when((r * cols_axis + target) // rows_axis == c)
            def _():
                act(own_copy(q, target))

    for q in range(chunks):
        load(q).start()
    stage_copy(0).start()
    barrier = pltpu.get_barrier_semaphore()
    for shift in range(1, cols_axis):
        pl.semaphore_signal(barrier, inc=1, device_id={"col": (c + shift) % cols_axis}, device_id_type=MESH)

    @pl.when(r >= 1)
    def _():
        pl.semaphore_signal(barrier, inc=1, device_id={"row": r - 1}, device_id_type=MESH)

    @pl.when(r + 1 < rows_axis)
    def _():
        pl.semaphore_signal(barrier, inc=1, device_id={"row": r + 1}, device_id_type=MESH)

    inner = (r >= 1) & (r + 1 < rows_axis)

    @pl.when(inner)
    def _():
        pl.semaphore_wait(barrier, cols_axis + 1)

    @pl.when(jnp.logical_not(inner))
    def _():
        pl.semaphore_wait(barrier, cols_axis)

    for q in range(chunks):
        load(q).wait()

    def split_tile(i, carry):
        @pl.when(i + 1 < tiles)
        def _():
            stage_copy(i + 1).start()

        stage_copy(i).wait()
        at = pl.ds(pl.multiple_of(i * tile, tile), tile)
        value = stage[i % 2]
        high = value.astype(jnp.bfloat16)
        a_hi[at, :] = high
        a_lo[at, :] = (value - high.astype(jnp.float32)).astype(jnp.bfloat16)
        return carry

    def multiply(k, i):
        even = 1 - 2 * (c % 2)
        target = (c + cols_axis // 2 + even * i + cols_axis) % cols_axis
        at = pl.ds(pl.multiple_of(target * rows, rows), rows)
        high = a_hi[at, :]
        out = jnp.dot(high, p_hi[...], preferred_element_type=jnp.float32)
        out += jnp.dot(high, p_lo[...], preferred_element_type=jnp.float32)
        out += jnp.dot(a_lo[at, :], p_hi[...], preferred_element_type=jnp.float32)
        partial[k, target] = out

        @pl.when(target != c)
        def _():
            part(k, target, c).start()

    def step(u, carry):
        q, p = u // pieces, u % pieces
        s, h = p // 2, p % 2

        @pl.when((u >= 2) & (u < chunks * pieces + 2))
        def _():
            v = u - 2
            wait_arrivals(v // pieces, (v % pieces) // 2, v % 2)

        @pl.when(q < chunks)
        def _():
            each_send(q, s, h, lambda copy: copy.start())

        @pl.when((q < chunks) & (p == 0))
        def _():
            own_of_block(q, r)

        @pl.when(u == 1)
        def _():
            lax.fori_loop(0, tiles, split_tile, 0)

        @pl.when((q >= 1) & (p == 1))
        def _():
            k = q - 1

            @pl.when(own_root == c)
            def _():
                own_here(k).start()

            def split_panel(b, carry):
                at = pl.ds(pl.multiple_of(b * rows, rows), rows)
                value = gathered[k, b]
                high = value.astype(jnp.bfloat16)
                p_hi[at, :] = high
                p_lo[at, :] = (value - high.astype(jnp.float32)).astype(jnp.bfloat16)
                return carry

            lax.fori_loop(0, rows_axis, split_panel, 0)

        @pl.when((q >= 1) & (p >= 1))
        def _():
            def body(i, carry):
                multiply(q - 1, i)
                return carry

            lax.fori_loop((p - 1) * cols_axis // (pieces - 1), p * cols_axis // (pieces - 1), body, 0)

        return carry

    lax.fori_loop(0, (chunks + 1) * pieces, step, 0)

    for q in range(chunks):
        panel, start = q // per_panel, (q % per_panel) * width
        at = (panel, slice(None), slice(start, start + width))
        total = partial[q, c]
        for shift in range(1, cols_axis):
            source = (c + shift) % cols_axis
            part(q, source, source).wait_recv()
            total += received[q, source]
        y_ref[at] = total

        @pl.when(own_root == c)
        def _():
            own_here(q).wait()

        @pl.when(own_root != c)
        def _():
            own_copy(q, own_root).wait_recv()

        own_ref[at] = own[q]

    def drain(u, carry):
        q, p = u // pieces, u % pieces
        each_send(q, p // 2, p % 2, lambda copy: copy.wait_send())
        return carry

    lax.fori_loop(0, chunks * pieces, drain, 0)
    for q in range(chunks):
        each_own(q, lambda copy: copy.wait_send())
        for shift in range(1, cols_axis):
            part(q, (c + shift) % cols_axis, c).wait_send()


def products(inverse_tile, masked):
    rows_axis, cols_axis = lax.axis_size("row"), lax.axis_size("col")
    height, depth = inverse_tile.shape
    count, rows, columns = masked.shape
    width = min(256, columns)
    chunks = count * columns // width
    tile = min(128, height)
    f32, bf16 = jnp.float32, jnp.bfloat16
    dma = pltpu.SemaphoreType.DMA
    result = jax.ShapeDtypeStruct((count, rows, columns), f32)
    return pl.pallas_call(
        functools.partial(exchange, (rows_axis, cols_axis), chunks),
        out_shape=(result, result),
        in_specs=[pl.BlockSpec(memory_space=pl.ANY)] * 2,
        out_specs=[pl.BlockSpec(memory_space=pltpu.VMEM)] * 2,
        scratch_shapes=[
            pltpu.VMEM((height, depth), bf16),
            pltpu.VMEM((height, depth), bf16),
            pltpu.VMEM((2, tile, depth), f32),
            pltpu.VMEM((depth, width), bf16),
            pltpu.VMEM((depth, width), bf16),
            pltpu.VMEM((chunks, rows_axis, rows, width), f32),
            pltpu.VMEM((chunks, cols_axis, rows, width), f32),
            pltpu.VMEM((chunks, cols_axis, rows, width), f32),
            pltpu.VMEM((chunks, rows, width), f32),
            dma((2,)),
            dma((chunks,)),
            dma((2, chunks, rows_axis, 2)),
            dma((chunks, rows_axis, 2)),
            dma((chunks, cols_axis)),
            dma((chunks, cols_axis)),
            dma((chunks, cols_axis)),
            dma((chunks,)),
            dma((chunks,)),
        ],
        compiler_params=pltpu.CompilerParams(
            collective_id=0, has_side_effects=True, vmem_limit_bytes=60 * 1024 * 1024),
    )(inverse_tile, masked)


def halving_levels():
    levels = []
    for axis in ("col", "row"):
        dist = 1
        while dist < lax.axis_size(axis):
            levels.append((axis, dist))
            dist *= 2
    return levels


def split(value):
    high = value.astype(jnp.bfloat16)
    return high, (value - high.astype(jnp.float32)).astype(jnp.bfloat16)


def dot3(a, b, contract):
    def one(left, right):
        return lax.dot_general(
            left, right, (((contract,), (0,)), ((), ())), preferred_element_type=jnp.float32)

    return one(a[0], b[0]) + (one(a[0], b[1]) + one(a[1], b[0]))


def finish_kernel(levels, count, y_ref, own_ref, link_ref, given_ref, anc_ref, diag_ref, cross_ref, terms, out_ref, *scratch):
    depth = len(levels)
    height, span = given_ref.shape[1:]
    rows_axis, cols_axis = terms.shape[3], 2 * terms.shape[1]
    kept = (terms,) + scratch[: depth - 1]
    landed = scratch[depth - 1 : 2 * depth - 1]
    send_sem, recv_sem = scratch[2 * depth - 1 :]

    def bit_and_partner(level):
        axis, dist = levels[level]
        at = lax.axis_index(axis)
        bit = (at // dist) % 2
        return bit, {axis: at + dist * (1 - 2 * bit)}

    def copy(level, k):
        bit, partner = bit_and_partner(level)
        return pltpu.make_async_remote_copy(
            kept[level].at[k, :, 1 - bit], landed[level].at[k], send_sem.at[level, k], recv_sem.at[level, k],
            device_id=partner, device_id_type=MESH)

    barrier = pltpu.get_barrier_semaphore()
    for level in range(depth):
        pl.semaphore_signal(barrier, inc=1, device_id=bit_and_partner(level)[1], device_id_type=MESH)
    pl.semaphore_wait(barrier, depth)

    def store(k, value):
        for col in range(cols_axis):
            for row in range(rows_axis):
                terms[k, col // 2, col % 2, row] = value[
                    row * height : (row + 1) * height, col * span : (col + 1) * span]

    row_id, col_id = lax.axis_index("row"), lax.axis_index("col")
    y1 = -y_ref[0]
    anc_ref[0] = y1
    first, y1_parts = split(own_ref[0]), split(y1)
    store(0, dot3(first, y1_parts, 0))
    copy(0, 0).start()
    link = split(link_ref[...])
    link_cols = link_ref[pl.ds(pl.multiple_of(col_id * span, span), span), :]
    link_rows = link_ref[pl.ds(pl.multiple_of(row_id * height, height), height), :]
    given = dot3(split(given_ref[0]), split(link_cols), 1)
    y2 = -(y_ref[1] + dot3(y1_parts, link, 1))
    anc_ref[1] = y2
    y2_parts = split(y2)
    store(1, dot3(first, y2_parts, 0))
    for col in range(cols_axis):
        terms[1, col // 2, col % 2, row_id] += given[:, col * span : (col + 1) * span]
    copy(0, 1).start()
    shifted = split(own_ref[1] - dot3(first, link, 1))
    store(2, dot3(shifted, y2_parts, 0) - dot3(split(link_rows), split(given), 0))
    copy(0, 2).start()

    for level in range(1, depth + 1):
        for k in range(count):
            copy(level - 1, k).wait_recv()
            bit, _ = bit_and_partner(level - 1)
            total = kept[level - 1][k, :, bit] + landed[level - 1][k]
            target = kept[level] if level < depth else out_ref
            target[k] = total.reshape(target.shape[1:])
            if level < depth:
                copy(level, k).start()
    diag_ref[0] = given_ref[0] - out_ref[0]
    diag_ref[1] = given_ref[1] - out_ref[2]
    cross_ref[...] = -out_ref[1]
    for level in range(depth):
        for k in range(count):
            copy(level, k).wait_send()


def finish(y, own, link, given):
    rows_axis, cols_axis = lax.axis_size("row"), lax.axis_size("col")
    count = 3
    height, span = given.shape[1:]
    levels = halving_levels()
    shapes = []
    cols, rows = cols_axis, rows_axis
    for axis, _ in levels:
        if axis == "col":
            cols //= 2
            shapes.append(((cols, 2, rows, height, span), (cols, rows, height, span)))
        else:
            rows //= 2
            shapes.append(((rows, 2, height, span), (rows, height, span)))
    dma = pltpu.SemaphoreType.DMA((len(levels), count))
    return pl.pallas_call(
        functools.partial(finish_kernel, levels, count),
        out_shape=(
            jax.ShapeDtypeStruct(y.shape, jnp.float32),
            jax.ShapeDtypeStruct(given.shape, jnp.float32),
            jax.ShapeDtypeStruct((height, span), jnp.float32),
        ),
        in_specs=[pl.BlockSpec(memory_space=pltpu.VMEM)] * 4,
        out_specs=[pl.BlockSpec(memory_space=pltpu.VMEM)] * 3,
        scratch_shapes=[
            pltpu.VMEM((count,) + shapes[0][0], jnp.float32),
            pltpu.VMEM((count, height, span), jnp.float32),
        ]
        + [pltpu.VMEM((count,) + kept, jnp.float32) for kept, _ in shapes[1:]]
        + [pltpu.VMEM((count,) + landed, jnp.float32) for _, landed in shapes]
        + [dma, dma],
        compiler_params=pltpu.CompilerParams(
            collective_id=1, has_side_effects=True, vmem_limit_bytes=48 * 1024 * 1024),
    )(y, own, link, given)


def order_of(r, count, i):
    near = jnp.minimum(r, count - 1 - r)
    close = r + ((i + 1) // 2) * (1 - 2 * (i % 2))
    far = jnp.where(2 * r < count - 1, r + i - near, r - i + near)
    return jnp.where(i <= 2 * near, close, far)


def fused_kernel(axis_sizes, tiles_ref, a_hbm, x_hbm, link_hbm, given_hbm, anc_ref, diag_ref, cross_ref,
                 a_hi, a_lo, stage, pieces, gathered, partial, pair_in, group_in, own, link, given, shift_x, shift_y,
                 given_link, term, term_pair, term_group, term_row,
                 stage_sem, load_sem, small_sem, hop_send, hop_recv, pair_send, pair_recv, group_send, group_recv,
                 own_send, own_recv, tp_send, tp_recv, tg_send, tg_recv, tr_send, tr_recv,
                 corner, corner_pair, corner_group, corner_row, cp_sem, cg_send, cg_recv, cr_send, cr_recv):
    rows_axis, cols_axis = axis_sizes
    groups = cols_axis // 2
    r = lax.axis_index("row")
    c = lax.axis_index("col")
    g, k = c // 2, c % 2
    chunks, _, rows, width = gathered.shape
    height, span = given.shape[1:]
    tile = stage.shape[1]
    tiles = a_hbm.shape[0] // tile
    last = chunks - 1
    end = cols_axis - 1

    def remote(src, dst, send, recv, **where):
        return pltpu.make_async_remote_copy(src, dst, send, recv, device_id=where, device_id_type=MESH)

    def load(q):
        src = x_hbm.at[q // cols_axis, :, pl.ds(pl.multiple_of((q % cols_axis) * width, width), width)]
        return pltpu.make_async_copy(src, gathered.at[q, r], load_sem.at[q])

    def stage_copy(i):
        src = a_hbm.at[pl.ds(pl.multiple_of(i * tile, tile), tile)]
        return pltpu.make_async_copy(src, stage.at[i % 2], stage_sem.at[i % 2])

    def hop(q, block, way, target):
        ref = gathered.at[q, block]
        return remote(ref, ref, hop_send.at[way, q, block], hop_recv.at[q, block], row=target)

    def send_own_block(q):
        @pl.when((r + 1 < rows_axis) & ((q < last) | (r >= c)))
        def _():
            hop(q, r, 0, r + 1).start()

        @pl.when((r >= 1) & ((q < last) | (r <= c)))
        def _():
            hop(q, r, 1, r - 1).start()

    def send_early():
        @pl.when(r < c)
        def _():
            hop(last, r, 0, r + 1).start()

        @pl.when(r > c)
        def _():
            hop(last, r, 1, r - 1).start()

    def pass_early(distance):
        @pl.when((r - distance >= 0) & (r <= c))
        def _():
            block = r - distance
            hop(last, block, 0, r - 1).wait_recv()

            @pl.when(r < c)
            def _():
                hop(last, block, 0, r + 1).start()

            @pl.when(r == c)
            def _():
                own_copy(last, block).start()

        @pl.when((r + distance < rows_axis) & (r >= c))
        def _():
            block = r + distance
            hop(last, block, 1, r + 1).wait_recv()

            @pl.when(r > c)
            def _():
                hop(last, block, 1, r - 1).start()

            @pl.when(r == c)
            def _():
                own_copy(last, block).start()

    def wait_and_forward(q, block):
        @pl.when((block < r) & ((q < last) | (r > c)))
        def _():
            hop(q, block, 0, r - 1).wait_recv()

        @pl.when((block > r) & ((q < last) | (r < c)))
        def _():
            hop(q, block, 1, r + 1).wait_recv()

        @pl.when((block < r) & (r + 1 < rows_axis) & ((q < last) | (r >= c)))
        def _():
            hop(q, block, 0, r + 1).start()

        @pl.when((block > r) & (r >= 1) & ((q < last) | (r <= c)))
        def _():
            hop(q, block, 1, r - 1).start()

    def pair_copy(q, t):
        return remote(partial.at[q, 2 * t + 1 - k], pair_in.at[q, t], pair_send.at[q, t], pair_recv.at[q, t],
                      col=c + 1 - 2 * k)

    def group_copy(q, shift):
        target = 2 * ((g + shift) % groups) + k
        return remote(partial.at[q, target], group_in.at[q, shift - 1], group_send.at[q, shift - 1],
                      group_recv.at[q, shift - 1], col=target)

    def own_copy(q, target):
        return remote(gathered.at[q, target], own.at[q], own_send.at[q, target], own_recv.at[q], col=target)

    def own_ready(q):
        @pl.when(r == c)
        def _():
            own[q] = gathered[q, c]

        @pl.when(r != c)
        def _():
            own_copy(q, c).wait_recv()

    def tp_copy(n, j):
        return remote(term.at[n, j], term_pair.at[n, j // 2], tp_send.at[n, j], tp_recv.at[n, j],
                      col=c + 1 - 2 * k)

    def tg_copy(n, j, shift):
        return remote(term.at[n, j], term_group.at[n, shift - 1], tg_send.at[n, j],
                      tg_recv.at[n, shift - 1], col=j)

    def tr_copy(n, target):
        return remote(term.at[n, c, target], term_row.at[n, r], tr_send.at[n, target],
                      tr_recv.at[n, r], row=target)

    def tr_wait(n, source):
        return remote(term.at[n, c, source], term_row.at[n, source], tr_send.at[n, source],
                      tr_recv.at[n, source], row=source)

    def term_start(n, j):
        @pl.when(j % 2 != k)
        def _():
            tp_copy(n, j).start()

    def term_mid(n, j):
        @pl.when(j % 2 == k)
        def _():
            tp_copy(n, j).wait_recv()
            term[n, j] += term_pair[n, j // 2]

            @pl.when(j != c)
            def _():
                tg_copy(n, j, (j // 2 - g + groups) % groups).start()

    def term_far(n, j):
        @pl.when(j == c)
        def _():
            total = term[n, j]
            for shift in range(1, groups):
                tg_copy(n, j, shift).wait_recv()
                total += term_group[n, shift - 1]
            term[n, j] = total

    def term_rows(n):
        for shift in range(1, rows_axis):
            tr_copy(n, (r + shift) % rows_axis).start()

    def term_end(n):
        total = term[n, c, r]
        for shift in range(1, rows_axis):
            source = (r + shift) % rows_axis
            tr_wait(n, source).wait_recv()
            total += term_row[n, source]
        return total

    def term_drain(n, j):
        @pl.when(j % 2 != k)
        def _():
            tp_copy(n, j).wait_send()

        @pl.when((j % 2 == k) & (j != c))
        def _():
            tg_copy(n, j, (j // 2 - g + groups) % groups).wait_send()

    def each_column(act, stop=cols_axis):
        def body(j, carry):
            act(j)
            return carry

        lax.fori_loop(0, stop, body, 0)

    def wide(ref, start, stop):
        return jnp.concatenate([ref[start + j] for j in range(stop)], axis=1)

    for q in range(chunks):
        load(q).start()
    small = [pltpu.make_async_copy(link_hbm, link, small_sem.at[0]),
             pltpu.make_async_copy(given_hbm, given, small_sem.at[1])]
    stage_copy(0).start()
    stage_copy(1).start()
    for copy in small:
        copy.start()
    barrier = pltpu.get_barrier_semaphore()
    for shift in range(1, cols_axis):
        pl.semaphore_signal(barrier, inc=1, device_id={"col": (c + shift) % cols_axis}, device_id_type=MESH)
    for shift in range(1, rows_axis):
        pl.semaphore_signal(barrier, inc=1, device_id={"row": (r + shift) % rows_axis}, device_id_type=MESH)

    per_block = rows // TILE
    first_tile = (c * rows_axis + r) * per_block

    def mask(q, carry):
        load(q).wait()
        for s in range(per_block):
            kept = (tiles_ref[q // cols_axis, first_tile + s] != 0).astype(jnp.float32)
            at = pl.ds(s * TILE, TILE)
            gathered[q, r, at] = gathered[q, r, at] * kept
        return carry

    lax.fori_loop(0, 2, mask, 0)
    pl.semaphore_wait(barrier, cols_axis + rows_axis - 2)
    send_own_block(0)
    send_own_block(1)
    lax.fori_loop(2, chunks, mask, 0)

    def split_tile(i, carry):
        stage_copy(i).wait()
        at = pl.ds(pl.multiple_of(i * tile, tile), tile)
        value = stage[i % 2]
        high = value.astype(jnp.bfloat16)
        a_hi[at, :] = high
        a_lo[at, :] = (value - high.astype(jnp.float32)).astype(jnp.bfloat16)

        @pl.when(i + 2 < tiles)
        def _():
            stage_copy(i + 2).start()

        return carry

    lax.fori_loop(0, tiles, split_tile, 0)

    def multiply(q, block, first, final=False):
        value = gathered[q, block]
        high = value.astype(jnp.bfloat16)
        pieces[:, :width] = high
        pieces[:, width:] = (value - high.astype(jnp.float32)).astype(jnp.bfloat16)
        inner = pl.ds(pl.multiple_of(block * rows, rows), rows)

        def body(i, carry):
            near = (g + 1 + i) % groups
            t = 2 * near + jnp.where(i < groups, 1 - k, k)
            at = pl.ds(pl.multiple_of(t * rows, rows), rows)
            both = jnp.dot(a_hi[at, inner], pieces[...], preferred_element_type=jnp.float32)
            out = jnp.dot(a_lo[at, inner], pieces[:, :width], preferred_element_type=jnp.float32)
            out += both[:, width:]
            out += both[:, :width]
            if first:
                partial[q, t] = out
            else:
                partial[q, t] += out
            if final:
                @pl.when(i < groups)
                def _():
                    pair_copy(q, near).start()

            return carry

        lax.fori_loop(0, cols_axis, body, 0)

    def pair_finish(q):
        for t in range(groups):
            pair_copy(q, t).wait_recv()
        for shift in range(1, groups):
            far = (g + shift) % groups
            partial[q, 2 * far + k] += pair_in[q, far]
            group_copy(q, shift).start()

    def total_of(q):
        total = partial[q, c] + pair_in[q, g]
        for shift in range(1, groups):
            group_copy(q, shift).wait_recv()
            total += group_in[q, shift - 1]
        return total

    def store_terms(n, value, j):
        for i in range(rows_axis):
            term[n, j, i] = value[i * height : (i + 1) * height]

    def first_done(_):
        for j in range(cols_axis):
            own_ready(j)
        y_parts = split(-anc_ref[0])
        x_parts = split(wide(own, 0, cols_axis))
        value = dot3(x_parts, y_parts, 0)
        for j in range(cols_axis):
            store_terms(0, value[:, j * span : (j + 1) * span], j)
        each_column(lambda j: term_start(0, j))
        for copy in small:
            copy.wait()
        link_parts = split(link[...])
        value = dot3(y_parts, link_parts, 1)
        for j in range(cols_axis):
            shift_y[j] = value[:, j * width : (j + 1) * width]
        value = dot3(x_parts, link_parts, 1)
        for j in range(cols_axis):
            shift_x[j] = value[:, j * width : (j + 1) * width]
        link_cols = link[pl.ds(pl.multiple_of(c * span, span), span), :]
        value = dot3(split(given[0]), split(link_cols), 1)
        for j in range(cols_axis):
            given_link[j] = value[:, j * span : (j + 1) * span]

    def own_shifted(j):
        own_ready(cols_axis + j)
        own[cols_axis + j] -= shift_x[j]

    def cross_term(j):
        value = dot3(split(anc_ref[0]), split(own[cols_axis + j]), 0)
        store_terms(1, -value, j)
        term[1, j, r] -= given_link[j]
        term_start(1, j)

    def second_chunk(j, total):
        value = shift_y[j] - total
        anc_ref[1, :, pl.ds(pl.multiple_of(j * width, width), width)] = value

    def second_terms():
        shifted = split(wide(own, cols_axis, cols_axis))
        done = split(anc_ref[1, :, : end * width])
        link_rows = link[pl.ds(pl.multiple_of(r * height, height), height), :]
        base = dot3(split(link_rows), split(wide(given_link, 0, cols_axis)), 0)
        value = dot3(shifted, done, 0)
        for j in range(end):
            at = slice(j * span, (j + 1) * span)
            store_terms(2, base[:, at] - value[:, at], j)
        value = dot3(done, split(own[last]), 0)
        for i in range(end):
            at = slice(i * height, (i + 1) * height)
            term[2, end, i] = base[at, end * span :] - value[at]
        term[2, end, end] = base[end * height :, end * span :]
        each_column(lambda j: term_start(2, j))

    def chunk(q, carry):
        prior = q - 1

        @pl.when(q + 2 <= last)
        def _():
            send_own_block(q + 2)

        @pl.when(q == end - 1)
        def _():
            send_early()

        multiply(q, r, True)

        @pl.when(q >= 1)
        def _():
            pair_finish(prior)

        for i in range(1, rows_axis):
            block = order_of(r, rows_axis, i)
            if i == rows_axis - 1:
                @pl.when(q == cols_axis + 1)
                def _():
                    each_column(lambda j: term_far(0, j))

                @pl.when(q >= cols_axis + 2)
                def _():
                    term_far(1, q - cols_axis - 2)

                @pl.when(q == last)
                def _():
                    term_far(1, end)
                    term_mid(1, end - 1)
                    each_column(lambda j: term_mid(2, j))

            wait_and_forward(q, block)

            @pl.when((r == c) & (q < last))
            def _():
                own_copy(q, block).start()

            multiply(q, block, False, i == rows_axis - 1)
            if i == 1:
                @pl.when((q >= end) & (q < end + rows_axis - 1))
                def _():
                    pass_early(q - end + 1)

                @pl.when(q == cols_axis + 1)
                def _():
                    each_column(lambda j: term_mid(0, j))

                @pl.when(q >= cols_axis + 2)
                def _():
                    term_mid(1, q - cols_axis - 2)

                @pl.when(q == last)
                def _():
                    term_mid(1, end)

            if i == 2:
                @pl.when((q >= 1) & (q <= cols_axis))
                def _():
                    at = pl.ds(pl.multiple_of(prior * width, width), width)
                    anc_ref[0, :, at] = -total_of(prior)

                @pl.when(q == cols_axis)
                def _():
                    first_done(None)

                @pl.when(q >= cols_axis + 1)
                def _():
                    j = prior - cols_axis
                    second_chunk(j, total_of(prior))
                    own_shifted(j)
                    cross_term(j)

                @pl.when(q == last - 1)
                def _():
                    own_shifted(end)
                    cross_term(end)

                @pl.when(q == last)
                def _():
                    second_terms()

        return carry

    lax.fori_loop(0, chunks, chunk, 0)

    term_rows(0)

    @pl.when(c != end - 1)
    def _():
        term_rows(1)

    pair_finish(last)
    term_far(1, end - 1)

    @pl.when(c == end - 1)
    def _():
        term_rows(1)

    each_column(lambda j: term_far(2, j))
    term_rows(2)
    second_chunk(end, total_of(last))
    corner[...] = -dot3(split(own[last]), split(anc_ref[1, :, end * width :]), 0)
    side, odd = end // 2, end % 2
    to_pair = remote(corner, corner_pair, cp_sem.at[0], cp_sem.at[1], col=c + 1 - 2 * k)

    def to_group(shift):
        return remote(corner, corner_group.at[shift - 1], cg_send, cg_recv.at[shift - 1], col=end)

    def to_row(source):
        return remote(corner, corner_row.at[source], cr_send, cr_recv.at[source], row=end)

    @pl.when(k != odd)
    def _():
        to_pair.start()

    diag_ref[0] = given[0] + term_end(0)
    cross_ref[...] = term_end(1)

    @pl.when(k == odd)
    def _():
        to_pair.wait_recv()
        corner[...] += corner_pair[...]

        @pl.when(g != side)
        def _():
            to_group((side - g + groups) % groups).start()

    diag_ref[1] = given[1] + term_end(2)

    @pl.when(c == end)
    def _():
        total = corner[...]
        for shift in range(1, groups):
            to_group(shift).wait_recv()
            total += corner_group[shift - 1]
        corner[...] = total

        @pl.when(r != end)
        def _():
            to_row(r).start()

        @pl.when(r == end)
        def _():
            total = diag_ref[1] + corner[...]
            for source in range(end):
                to_row(source).wait_recv()
                total += corner_row[source]
            diag_ref[1] = total

    @pl.when(k != odd)
    def _():
        to_pair.wait_send()

    @pl.when((k == odd) & (g != side))
    def _():
        to_group((side - g + groups) % groups).wait_send()

    @pl.when((c == end) & (r != end))
    def _():
        to_row(r).wait_send()

    def drain(q, carry):
        def body(block, carry):
            @pl.when((block <= r) & (r + 1 < rows_axis))
            def _():
                hop(q, block, 0, r + 1).wait_send()

            @pl.when((block >= r) & (r >= 1))
            def _():
                hop(q, block, 1, r - 1).wait_send()

            return carry

        lax.fori_loop(0, rows_axis, body, 0)
        for shift in range(1, cols_axis):
            @pl.when(r == c)
            def _():
                own_copy(q, (c + shift) % cols_axis).wait_send()

        for t in range(groups):
            pair_copy(q, t).wait_send()
        for shift in range(1, groups):
            group_copy(q, shift).wait_send()
        return carry

    lax.fori_loop(0, chunks, drain, 0)
    for n in range(3):
        each_column(lambda j: term_drain(n, j))
        for shift in range(1, rows_axis):
            tr_copy(n, (r + shift) % rows_axis).wait_send()


def fused(inverse_tile, panels, link_panel, given, tiles):
    rows_axis, cols_axis = lax.axis_size("row"), lax.axis_size("col")
    groups = cols_axis // 2
    full, depth = inverse_tile.shape
    count, rows, columns = panels.shape
    height, span = given.shape[1:]
    width = span
    chunks = count * cols_axis
    tile = min(128, full)
    f32, bf16 = jnp.float32, jnp.bfloat16
    dma = pltpu.SemaphoreType.DMA
    vmem = pltpu.VMEM
    return pl.pallas_call(
        functools.partial(fused_kernel, (rows_axis, cols_axis)),
        out_shape=(
            jax.ShapeDtypeStruct((count, rows, columns), f32),
            jax.ShapeDtypeStruct(given.shape, f32),
            jax.ShapeDtypeStruct((height, span), f32),
        ),
        in_specs=[pl.BlockSpec(memory_space=pltpu.SMEM)] + [pl.BlockSpec(memory_space=pl.ANY)] * 4,
        out_specs=[pl.BlockSpec(memory_space=vmem)] * 3,
        scratch_shapes=[
            vmem((full, depth), bf16),
            vmem((full, depth), bf16),
            vmem((2, tile, depth), f32),
            vmem((rows, 2 * width), bf16),
            vmem((chunks, rows_axis, rows, width), f32),
            vmem((chunks, cols_axis, rows, width), f32),
            vmem((chunks, groups, rows, width), f32),
            vmem((chunks, max(groups - 1, 1), rows, width), f32),
            vmem((chunks, rows, width), f32),
            vmem((columns, columns), f32),
            vmem(given.shape, f32),
            vmem((cols_axis, rows, width), f32),
            vmem((cols_axis, rows, width), f32),
            vmem((cols_axis, height, span), f32),
            vmem((3, cols_axis, rows_axis, height, span), f32),
            vmem((3, groups, rows_axis, height, span), f32),
            vmem((3, max(groups - 1, 1), rows_axis, height, span), f32),
            vmem((3, rows_axis, height, span), f32),
            dma((2,)),
            dma((chunks,)),
            dma((2,)),
            dma((2, chunks, rows_axis)),
            dma((chunks, rows_axis)),
            dma((chunks, groups)),
            dma((chunks, groups)),
            dma((chunks, max(groups - 1, 1))),
            dma((chunks, max(groups - 1, 1))),
            dma((chunks, cols_axis)),
            dma((chunks,)),
            dma((3, cols_axis)),
            dma((3, cols_axis)),
            dma((3, cols_axis)),
            dma((3, max(groups - 1, 1))),
            dma((3, rows_axis)),
            dma((3, rows_axis)),
            vmem((height, span), f32),
            vmem((height, span), f32),
            vmem((max(groups - 1, 1), height, span), f32),
            vmem((rows_axis, height, span), f32),
            dma((2,)),
            dma,
            dma((max(groups - 1, 1),)),
            dma,
            dma((rows_axis,)),
        ],
        compiler_params=pltpu.CompilerParams(
            collective_id=2, has_side_effects=True, vmem_limit_bytes=58 * 1024 * 1024),
    )(tiles, inverse_tile, panels, link_panel, given)


def local(inverse_tile, panels, link_panel, diag_inverse, ancestor_tiles):
    rows_axis, cols_axis = lax.axis_size("row"), lax.axis_size("col")
    rows, columns = panels.shape[2:]
    square = rows_axis == cols_axis >= 4 and cols_axis % 2 == 0 and rows % TILE == 0 and (columns // cols_axis) % 128 == 0
    if square:
        anc, diag, cross = fused(inverse_tile, panels[0], link_panel[0], diag_inverse[0], ancestor_tiles[0])
    else:
        masked = mask_panels(panels, ancestor_tiles)[0]
        ys, own = products(inverse_tile, masked)
        anc, diag, cross = finish(ys, own, link_panel[0], diag_inverse[0])
    return anc[None], diag[None], cross[None]


def solution(mesh):
    in_specs = (
        P(("hyp", "row"), "col"),
        P("hyp", None, ("col", "row"), None),
        P("hyp", None, None),
        P("hyp", None, "row", "col"),
        P(),
    )
    out_specs = (
        P("hyp", None, ("row", "col"), None),
        P("hyp", None, "row", "col"),
        P("hyp", "row", "col"),
    )
    return jax.shard_map(local, mesh=mesh, in_specs=in_specs, out_specs=out_specs, check_vma=False)
```

```python
import functools

import jax
import jax.numpy as jnp
from jax import lax
from jax.experimental import pallas as pl
from jax.experimental.pallas import tpu as pltpu
from jax.sharding import PartitionSpec as P

TILE = 128
MESH = pl.DeviceIdType.MESH


def mask_panels(panels, ancestor_tiles):
    rows_axis = lax.axis_size("row")
    local_rows = panels.shape[2]
    row_start = (lax.axis_index("col") * rows_axis + lax.axis_index("row")) * local_rows
    tile_mask = jnp.repeat(ancestor_tiles, TILE, axis=2)
    kept_rows = lax.dynamic_slice_in_dim(tile_mask, row_start, local_rows, 2)
    return jnp.where(kept_rows[..., None] != 0, panels, 0.0)


def exchange(axis_sizes, chunks, a_hbm, x_hbm, y_ref, own_ref, a_hi, a_lo, stage, p_hi, p_lo, gathered, partial,
             received, own, stage_sem, load_sem, send_sem, recv_sem, part_send, part_recv, own_send, own_recv, own_local):
    rows_axis, cols_axis = axis_sizes
    r = lax.axis_index("row")
    c = lax.axis_index("col")
    _, _, rows, width = gathered.shape
    half = rows // 2
    per_panel = chunks // x_hbm.shape[0]
    pieces = 2 * (rows_axis - 1)
    tile = stage.shape[1]
    tiles = a_hbm.shape[0] // tile

    def load(q):
        src = x_hbm.at[q // per_panel, :, pl.ds((q % per_panel) * width, width)]
        return pltpu.make_async_copy(src, gathered.at[q, r], load_sem.at[q])

    def stage_copy(i):
        src = a_hbm.at[pl.ds(pl.multiple_of(i * tile, tile), tile)]
        return pltpu.make_async_copy(src, stage.at[i % 2], stage_sem.at[i % 2])

    def hop(q, block, h, way, target):
        ref = gathered.at[q, block, pl.ds(pl.multiple_of(h * half, half), half)]
        return pltpu.make_async_remote_copy(
            ref, ref, send_sem.at[way, q, block, h], recv_sem.at[q, block, h],
            device_id={"row": target}, device_id_type=MESH)

    def each_send(q, s, h, act):
        @pl.when((r + 1 < rows_axis) & (r - s >= 0))
        def _():
            act(hop(q, r - s, h, 0, r + 1))

        @pl.when((r >= 1) & (r + s < rows_axis))
        def _():
            act(hop(q, r + s, h, 1, r - 1))

    def wait_arrivals(q, s, h):
        @pl.when(r - 1 - s >= 0)
        def _():
            hop(q, r - 1 - s, h, 0, r - 1).wait_recv()

            @pl.when(h == 1)
            def _():
                own_of_block(q, r - 1 - s)

        @pl.when(r + 1 + s < rows_axis)
        def _():
            hop(q, r + 1 + s, h, 1, r + 1).wait_recv()

            @pl.when(h == 1)
            def _():
                own_of_block(q, r + 1 + s)

    def part(q, target, source):
        return pltpu.make_async_remote_copy(
            partial.at[q, target], received.at[q, source], part_send.at[q, target], part_recv.at[q, source],
            device_id={"col": target}, device_id_type=MESH)

    def own_copy(q, target):
        return pltpu.make_async_remote_copy(
            gathered.at[q, (r * cols_axis + target) % rows_axis], own.at[q], own_send.at[q, target], own_recv.at[q],
            device_id={"col": target}, device_id_type=MESH)

    def own_here(q):
        return pltpu.make_async_copy(gathered.at[q, (r * cols_axis + c) % rows_axis], own.at[q], own_local.at[q])

    own_root = (r * cols_axis + c) // rows_axis

    def own_of_block(q, block):
        for shift in range(1, cols_axis):
            target = (c + shift) % cols_axis
            place = r * cols_axis + target

            @pl.when((place // rows_axis == c) & (place % rows_axis == block))
            def _():
                own_copy(q, target).start()

    def each_own(q, act):
        for shift in range(1, cols_axis):
            target = (c + shift) % cols_axis

            @pl.when((r * cols_axis + target) // rows_axis == c)
            def _():
                act(own_copy(q, target))

    for q in range(chunks):
        load(q).start()
    stage_copy(0).start()
    barrier = pltpu.get_barrier_semaphore()
    for shift in range(1, cols_axis):
        pl.semaphore_signal(barrier, inc=1, device_id={"col": (c + shift) % cols_axis}, device_id_type=MESH)

    @pl.when(r >= 1)
    def _():
        pl.semaphore_signal(barrier, inc=1, device_id={"row": r - 1}, device_id_type=MESH)

    @pl.when(r + 1 < rows_axis)
    def _():
        pl.semaphore_signal(barrier, inc=1, device_id={"row": r + 1}, device_id_type=MESH)

    inner = (r >= 1) & (r + 1 < rows_axis)

    @pl.when(inner)
    def _():
        pl.semaphore_wait(barrier, cols_axis + 1)

    @pl.when(jnp.logical_not(inner))
    def _():
        pl.semaphore_wait(barrier, cols_axis)

    for q in range(chunks):
        load(q).wait()

    def split_tile(i, carry):
        @pl.when(i + 1 < tiles)
        def _():
            stage_copy(i + 1).start()

        stage_copy(i).wait()
        at = pl.ds(pl.multiple_of(i * tile, tile), tile)
        value = stage[i % 2]
        high = value.astype(jnp.bfloat16)
        a_hi[at, :] = high
        a_lo[at, :] = (value - high.astype(jnp.float32)).astype(jnp.bfloat16)
        return carry

    def multiply(k, i):
        even = 1 - 2 * (c % 2)
        target = (c + cols_axis // 2 + even * i + cols_axis) % cols_axis
        at = pl.ds(pl.multiple_of(target * rows, rows), rows)
        high = a_hi[at, :]
        out = jnp.dot(high, p_hi[...], preferred_element_type=jnp.float32)
        out += jnp.dot(high, p_lo[...], preferred_element_type=jnp.float32)
        out += jnp.dot(a_lo[at, :], p_hi[...], preferred_element_type=jnp.float32)
        partial[k, target] = out

        @pl.when(target != c)
        def _():
            part(k, target, c).start()

    def step(u, carry):
        q, p = u // pieces, u % pieces
        s, h = p // 2, p % 2

        @pl.when((u >= 2) & (u < chunks * pieces + 2))
        def _():
            v = u - 2
            wait_arrivals(v // pieces, (v % pieces) // 2, v % 2)

        @pl.when(q < chunks)
        def _():
            each_send(q, s, h, lambda copy: copy.start())

        @pl.when((q < chunks) & (p == 0))
        def _():
            own_of_block(q, r)

        @pl.when(u == 1)
        def _():
            lax.fori_loop(0, tiles, split_tile, 0)

        @pl.when((q >= 1) & (p == 1))
        def _():
            k = q - 1

            @pl.when(own_root == c)
            def _():
                own_here(k).start()

            def split_panel(b, carry):
                at = pl.ds(pl.multiple_of(b * rows, rows), rows)
                value = gathered[k, b]
                high = value.astype(jnp.bfloat16)
                p_hi[at, :] = high
                p_lo[at, :] = (value - high.astype(jnp.float32)).astype(jnp.bfloat16)
                return carry

            lax.fori_loop(0, rows_axis, split_panel, 0)

        @pl.when((q >= 1) & (p >= 1))
        def _():
            def body(i, carry):
                multiply(q - 1, i)
                return carry

            lax.fori_loop((p - 1) * cols_axis // (pieces - 1), p * cols_axis // (pieces - 1), body, 0)

        return carry

    lax.fori_loop(0, (chunks + 1) * pieces, step, 0)

    for q in range(chunks):
        panel, start = q // per_panel, (q % per_panel) * width
        at = (panel, slice(None), slice(start, start + width))
        total = partial[q, c]
        for shift in range(1, cols_axis):
            source = (c + shift) % cols_axis
            part(q, source, source).wait_recv()
            total += received[q, source]
        y_ref[at] = total

        @pl.when(own_root == c)
        def _():
            own_here(q).wait()

        @pl.when(own_root != c)
        def _():
            own_copy(q, own_root).wait_recv()

        own_ref[at] = own[q]

    def drain(u, carry):
        q, p = u // pieces, u % pieces
        each_send(q, p // 2, p % 2, lambda copy: copy.wait_send())
        return carry

    lax.fori_loop(0, chunks * pieces, drain, 0)
    for q in range(chunks):
        each_own(q, lambda copy: copy.wait_send())
        for shift in range(1, cols_axis):
            part(q, (c + shift) % cols_axis, c).wait_send()


def products(inverse_tile, masked):
    rows_axis, cols_axis = lax.axis_size("row"), lax.axis_size("col")
    height, depth = inverse_tile.shape
    count, rows, columns = masked.shape
    width = min(256, columns)
    chunks = count * columns // width
    tile = min(128, height)
    f32, bf16 = jnp.float32, jnp.bfloat16
    dma = pltpu.SemaphoreType.DMA
    result = jax.ShapeDtypeStruct((count, rows, columns), f32)
    return pl.pallas_call(
        functools.partial(exchange, (rows_axis, cols_axis), chunks),
        out_shape=(result, result),
        in_specs=[pl.BlockSpec(memory_space=pl.ANY)] * 2,
        out_specs=[pl.BlockSpec(memory_space=pltpu.VMEM)] * 2,
        scratch_shapes=[
            pltpu.VMEM((height, depth), bf16),
            pltpu.VMEM((height, depth), bf16),
            pltpu.VMEM((2, tile, depth), f32),
            pltpu.VMEM((depth, width), bf16),
            pltpu.VMEM((depth, width), bf16),
            pltpu.VMEM((chunks, rows_axis, rows, width), f32),
            pltpu.VMEM((chunks, cols_axis, rows, width), f32),
            pltpu.VMEM((chunks, cols_axis, rows, width), f32),
            pltpu.VMEM((chunks, rows, width), f32),
            dma((2,)),
            dma((chunks,)),
            dma((2, chunks, rows_axis, 2)),
            dma((chunks, rows_axis, 2)),
            dma((chunks, cols_axis)),
            dma((chunks, cols_axis)),
            dma((chunks, cols_axis)),
            dma((chunks,)),
            dma((chunks,)),
        ],
        compiler_params=pltpu.CompilerParams(
            collective_id=0, has_side_effects=True, vmem_limit_bytes=60 * 1024 * 1024),
    )(inverse_tile, masked)


def halving_levels():
    levels = []
    for axis in ("col", "row"):
        dist = 1
        while dist < lax.axis_size(axis):
            levels.append((axis, dist))
            dist *= 2
    return levels


def split(value):
    high = value.astype(jnp.bfloat16)
    return high, (value - high.astype(jnp.float32)).astype(jnp.bfloat16)


def dot3(a, b, contract):
    def one(left, right):
        return lax.dot_general(
            left, right, (((contract,), (0,)), ((), ())), preferred_element_type=jnp.float32)

    return one(a[0], b[0]) + (one(a[0], b[1]) + one(a[1], b[0]))


def finish_kernel(levels, count, y_ref, own_ref, link_ref, given_ref, anc_ref, diag_ref, cross_ref, terms, out_ref, *scratch):
    depth = len(levels)
    height, span = given_ref.shape[1:]
    rows_axis, cols_axis = terms.shape[3], 2 * terms.shape[1]
    kept = (terms,) + scratch[: depth - 1]
    landed = scratch[depth - 1 : 2 * depth - 1]
    send_sem, recv_sem = scratch[2 * depth - 1 :]

    def bit_and_partner(level):
        axis, dist = levels[level]
        at = lax.axis_index(axis)
        bit = (at // dist) % 2
        return bit, {axis: at + dist * (1 - 2 * bit)}

    def copy(level, k):
        bit, partner = bit_and_partner(level)
        return pltpu.make_async_remote_copy(
            kept[level].at[k, :, 1 - bit], landed[level].at[k], send_sem.at[level, k], recv_sem.at[level, k],
            device_id=partner, device_id_type=MESH)

    barrier = pltpu.get_barrier_semaphore()
    for level in range(depth):
        pl.semaphore_signal(barrier, inc=1, device_id=bit_and_partner(level)[1], device_id_type=MESH)
    pl.semaphore_wait(barrier, depth)

    def store(k, value):
        for col in range(cols_axis):
            for row in range(rows_axis):
                terms[k, col // 2, col % 2, row] = value[
                    row * height : (row + 1) * height, col * span : (col + 1) * span]

    row_id, col_id = lax.axis_index("row"), lax.axis_index("col")
    y1 = -y_ref[0]
    anc_ref[0] = y1
    first, y1_parts = split(own_ref[0]), split(y1)
    store(0, dot3(first, y1_parts, 0))
    copy(0, 0).start()
    link = split(link_ref[...])
    link_cols = link_ref[pl.ds(pl.multiple_of(col_id * span, span), span), :]
    link_rows = link_ref[pl.ds(pl.multiple_of(row_id * height, height), height), :]
    given = dot3(split(given_ref[0]), split(link_cols), 1)
    y2 = -(y_ref[1] + dot3(y1_parts, link, 1))
    anc_ref[1] = y2
    y2_parts = split(y2)
    store(1, dot3(first, y2_parts, 0))
    for col in range(cols_axis):
        terms[1, col // 2, col % 2, row_id] += given[:, col * span : (col + 1) * span]
    copy(0, 1).start()
    shifted = split(own_ref[1] - dot3(first, link, 1))
    store(2, dot3(shifted, y2_parts, 0) - dot3(split(link_rows), split(given), 0))
    copy(0, 2).start()

    for level in range(1, depth + 1):
        for k in range(count):
            copy(level - 1, k).wait_recv()
            bit, _ = bit_and_partner(level - 1)
            total = kept[level - 1][k, :, bit] + landed[level - 1][k]
            target = kept[level] if level < depth else out_ref
            target[k] = total.reshape(target.shape[1:])
            if level < depth:
                copy(level, k).start()
    diag_ref[0] = given_ref[0] - out_ref[0]
    diag_ref[1] = given_ref[1] - out_ref[2]
    cross_ref[...] = -out_ref[1]
    for level in range(depth):
        for k in range(count):
            copy(level, k).wait_send()


def finish(y, own, link, given):
    rows_axis, cols_axis = lax.axis_size("row"), lax.axis_size("col")
    count = 3
    height, span = given.shape[1:]
    levels = halving_levels()
    shapes = []
    cols, rows = cols_axis, rows_axis
    for axis, _ in levels:
        if axis == "col":
            cols //= 2
            shapes.append(((cols, 2, rows, height, span), (cols, rows, height, span)))
        else:
            rows //= 2
            shapes.append(((rows, 2, height, span), (rows, height, span)))
    dma = pltpu.SemaphoreType.DMA((len(levels), count))
    return pl.pallas_call(
        functools.partial(finish_kernel, levels, count),
        out_shape=(
            jax.ShapeDtypeStruct(y.shape, jnp.float32),
            jax.ShapeDtypeStruct(given.shape, jnp.float32),
            jax.ShapeDtypeStruct((height, span), jnp.float32),
        ),
        in_specs=[pl.BlockSpec(memory_space=pltpu.VMEM)] * 4,
        out_specs=[pl.BlockSpec(memory_space=pltpu.VMEM)] * 3,
        scratch_shapes=[
            pltpu.VMEM((count,) + shapes[0][0], jnp.float32),
            pltpu.VMEM((count, height, span), jnp.float32),
        ]
        + [pltpu.VMEM((count,) + kept, jnp.float32) for kept, _ in shapes[1:]]
        + [pltpu.VMEM((count,) + landed, jnp.float32) for _, landed in shapes]
        + [dma, dma],
        compiler_params=pltpu.CompilerParams(
            collective_id=1, has_side_effects=True, vmem_limit_bytes=48 * 1024 * 1024),
    )(y, own, link, given)


def order_of(r, count, i):
    near = jnp.minimum(r, count - 1 - r)
    close = r + ((i + 1) // 2) * (1 - 2 * (i % 2))
    far = jnp.where(2 * r < count - 1, r + i - near, r - i + near)
    return jnp.where(i <= 2 * near, close, far)


def fused_kernel(axis_sizes, tiles_ref, a_hbm, x_hbm, link_hbm, given_hbm, anc_ref, diag_ref, cross_ref,
                 a_hi, a_lo, stage, pieces, gathered, partial, pair_in, group_in, own, link, given, shift_x, shift_y,
                 given_link, term, term_pair, term_group, term_row,
                 stage_sem, load_sem, small_sem, hop_send, hop_recv, pair_send, pair_recv, group_send, group_recv,
                 own_send, own_recv, tp_send, tp_recv, tg_send, tg_recv, tr_send, tr_recv,
                 chain_in, chain_send, chain_recv,
                 late, late_pair, late_group, late_row, lp_sem, lg_send, lg_recv, lr_send, lr_recv,
                 bottom, bottom_pair, bottom_group, bottom_row, bp_send, bp_recv, bg_send, bg_recv, br_send, br_recv):
    rows_axis, cols_axis = axis_sizes
    groups = cols_axis // 2
    r = lax.axis_index("row")
    c = lax.axis_index("col")
    g, k = c // 2, c % 2
    chunks, _, rows, width = gathered.shape
    height, span = given.shape[1:]
    tile = stage.shape[1]
    tiles = a_hbm.shape[0] // tile
    last = chunks - 1
    end = cols_axis - 1

    def remote(src, dst, send, recv, **where):
        return pltpu.make_async_remote_copy(src, dst, send, recv, device_id=where, device_id_type=MESH)

    def load(q):
        src = x_hbm.at[q // cols_axis, :, pl.ds(pl.multiple_of((q % cols_axis) * width, width), width)]
        return pltpu.make_async_copy(src, gathered.at[q, r], load_sem.at[q])

    def stage_copy(i):
        src = a_hbm.at[pl.ds(pl.multiple_of(i * tile, tile), tile)]
        return pltpu.make_async_copy(src, stage.at[i % 2], stage_sem.at[i % 2])

    def hop(q, block, way, target):
        ref = gathered.at[q, block]
        return remote(ref, ref, hop_send.at[way, q, block], hop_recv.at[q, block], row=target)

    def send_own_block(q):
        @pl.when((r + 1 < rows_axis))
        def _():
            hop(q, r, 0, r + 1).start()

        @pl.when((r >= 1))
        def _():
            hop(q, r, 1, r - 1).start()

    def wait_and_forward(q, block):
        @pl.when((block < r))
        def _():
            hop(q, block, 0, r - 1).wait_recv()

        @pl.when((block > r))
        def _():
            hop(q, block, 1, r + 1).wait_recv()

        @pl.when((block < r) & (r + 1 < rows_axis))
        def _():
            hop(q, block, 0, r + 1).start()

        @pl.when((block > r) & (r >= 1))
        def _():
            hop(q, block, 1, r - 1).start()

    def pair_copy(q, t):
        return remote(partial.at[q % 2, 2 * t + 1 - k], pair_in.at[q, t], pair_send.at[q, t], pair_recv.at[q, t],
                      col=c + 1 - 2 * k)

    def group_copy(q, shift):
        target = 2 * ((g + shift) % groups) + k
        return remote(partial.at[q % 2, target], group_in.at[q, shift - 1], group_send.at[q, shift - 1],
                      group_recv.at[q, shift - 1], col=target)

    def own_copy(q, target):
        return remote(gathered.at[q, target], own.at[q], own_send.at[q, target], own_recv.at[q], col=target)

    def own_ready(q):
        @pl.when(r == c)
        def _():
            own[q] = gathered[q, c]

        @pl.when(r != c)
        def _():
            own_copy(q, c).wait_recv()

    def part(n):
        return pl.ds(0, end if n == 2 else rows_axis)

    def tp_copy(n, j):
        return remote(term.at[n, j, part(n)], term_pair.at[n, j // 2, part(n)], tp_send.at[n, j], tp_recv.at[n, j],
                      col=c + 1 - 2 * k)

    def tg_copy(n, j, shift):
        return remote(term.at[n, j, part(n)], term_group.at[n, shift - 1, part(n)], tg_send.at[n, j],
                      tg_recv.at[n, shift - 1], col=j)

    def tr_copy(n, target):
        return remote(term.at[n, c, target], term_row.at[n, r], tr_send.at[n, target],
                      tr_recv.at[n, r], row=target)

    def tr_wait(n, source):
        return remote(term.at[n, c, source], term_row.at[n, source], tr_send.at[n, source],
                      tr_recv.at[n, source], row=source)

    def term_start(n, j):
        @pl.when(j % 2 != k)
        def _():
            tp_copy(n, j).start()

    def term_mid(n, j):
        @pl.when(j % 2 == k)
        def _():
            tp_copy(n, j).wait_recv()
            term[n, j] += term_pair[n, j // 2]

            @pl.when(j != c)
            def _():
                tg_copy(n, j, (j // 2 - g + groups) % groups).start()

    def term_far(n, j):
        @pl.when(j == c)
        def _():
            total = term[n, j]
            for shift in range(1, groups):
                tg_copy(n, j, shift).wait_recv()
                total += term_group[n, shift - 1]
            term[n, j] = total

    def each_row(n, act):
        for shift in range(1, rows_axis):
            target = (r + shift) % rows_axis
            wanted = c < end
            if n == 2:
                wanted = wanted & (target < end)

            @pl.when(wanted)
            def _():
                act(target)

    def term_rows(n):
        each_row(n, lambda target: tr_copy(n, target).start())

    def term_end(n):
        total = term[n, c, r]
        for shift in range(1, rows_axis):
            source = (r + shift) % rows_axis
            tr_wait(n, source).wait_recv()
            total += term_row[n, source]
        return total

    def chain_copy(way, target):
        return remote(term.at[0, c, target], chain_in.at[way, target], chain_send.at[way, target],
                      chain_recv.at[way, target], row=r + 1 - 2 * way)

    def chain(step):
        for way in range(2):
            at = step if way == 0 else rows_axis - 1 - step
            ahead = range(at + 1, rows_axis) if way == 0 else range(at)

            @pl.when(r == at)
            def _():
                if step > 0:
                    for target in [at, *ahead]:
                        chain_copy(way, target).wait_recv()
                        term[0, c, target] += chain_in[way, target]
                for target in ahead:
                    chain_copy(way, target).start()

    def chain_drain():
        for way in range(2):
            for target in range(rows_axis):
                @pl.when((target > r) if way == 0 else (target < r))
                def _():
                    chain_copy(way, target).wait_send()

    side, odd = end // 2, end % 2

    def lp_copy():
        return remote(late, late_pair, lp_sem.at[0], lp_sem.at[1], col=c + 1 - 2 * k)

    def lg_copy(shift):
        return remote(late, late_group.at[shift - 1], lg_send, lg_recv.at[shift - 1], col=end)

    def lr_copy(target, source):
        return remote(late.at[target], late_row.at[source], lr_send.at[target], lr_recv.at[source], row=target)

    def late_start():
        @pl.when(k != odd)
        def _():
            lp_copy().start()

    def late_mid():
        @pl.when(k == odd)
        def _():
            lp_copy().wait_recv()
            late[...] += late_pair[...]

            @pl.when(g != side)
            def _():
                lg_copy((side - g + groups) % groups).start()

    def late_far():
        @pl.when(c == end)
        def _():
            total = late[...]
            for shift in range(1, groups):
                lg_copy(shift).wait_recv()
                total += late_group[shift - 1]
            late[...] = total
            for shift in range(1, rows_axis):
                lr_copy((r + shift) % rows_axis, r).start()

    def late_drain():
        @pl.when(k != odd)
        def _():
            lp_copy().wait_send()

        @pl.when((k == odd) & (g != side))
        def _():
            lg_copy((side - g + groups) % groups).wait_send()

        @pl.when(c == end)
        def _():
            for shift in range(1, rows_axis):
                lr_copy((r + shift) % rows_axis, r).wait_send()

    def bp_copy(j):
        return remote(bottom.at[j], bottom_pair.at[j // 2], bp_send.at[j], bp_recv.at[j], col=c + 1 - 2 * k)

    def bg_copy(j, shift):
        return remote(bottom.at[j], bottom_group.at[shift - 1], bg_send.at[j], bg_recv.at[shift - 1], col=j)

    def br_copy(source):
        return remote(bottom.at[c], bottom_row.at[source], br_send, br_recv.at[source], row=end)

    def bottom_start(j):
        @pl.when(j % 2 != k)
        def _():
            bp_copy(j).start()

    def bottom_mid(j):
        @pl.when(j % 2 == k)
        def _():
            bp_copy(j).wait_recv()
            bottom[j] += bottom_pair[j // 2]

            @pl.when(j != c)
            def _():
                bg_copy(j, (j // 2 - g + groups) % groups).start()

    def bottom_far(j):
        @pl.when(j == c)
        def _():
            total = bottom[j]
            for shift in range(1, groups):
                bg_copy(j, shift).wait_recv()
                total += bottom_group[shift - 1]
            bottom[j] = total

            @pl.when(r != end)
            def _():
                br_copy(r).start()

    def bottom_drain(j):
        @pl.when(j % 2 != k)
        def _():
            bp_copy(j).wait_send()

        @pl.when((j % 2 == k) & (j != c))
        def _():
            bg_copy(j, (j // 2 - g + groups) % groups).wait_send()

        @pl.when((j == c) & (r != end))
        def _():
            br_copy(r).wait_send()

    def term_drain(n, j):
        @pl.when(j % 2 != k)
        def _():
            tp_copy(n, j).wait_send()

        @pl.when((j % 2 == k) & (j != c))
        def _():
            tg_copy(n, j, (j // 2 - g + groups) % groups).wait_send()

    def each_column(act, stop=cols_axis):
        def body(j, carry):
            act(j)
            return carry

        lax.fori_loop(0, stop, body, 0)

    def wide(ref, start, stop):
        return jnp.concatenate([ref[start + j] for j in range(stop)], axis=1)

    for q in range(chunks):
        load(q).start()
    small = [pltpu.make_async_copy(link_hbm, link, small_sem.at[0]),
             pltpu.make_async_copy(given_hbm, given, small_sem.at[1])]
    stage_copy(0).start()
    stage_copy(1).start()
    for copy in small:
        copy.start()
    barrier = pltpu.get_barrier_semaphore()
    for shift in range(1, cols_axis):
        pl.semaphore_signal(barrier, inc=1, device_id={"col": (c + shift) % cols_axis}, device_id_type=MESH)
    for shift in range(1, rows_axis):
        pl.semaphore_signal(barrier, inc=1, device_id={"row": (r + shift) % rows_axis}, device_id_type=MESH)

    per_block = rows // TILE
    first_tile = (c * rows_axis + r) * per_block

    def mask(q, carry):
        load(q).wait()
        for s in range(per_block):
            kept = (tiles_ref[q // cols_axis, first_tile + s] != 0).astype(jnp.float32)
            at = pl.ds(s * TILE, TILE)
            gathered[q, r, at] = gathered[q, r, at] * kept
        return carry

    lax.fori_loop(0, 2, mask, 0)
    pl.semaphore_wait(barrier, cols_axis + rows_axis - 2)
    send_own_block(0)
    send_own_block(1)
    lax.fori_loop(2, chunks, mask, 0)

    def split_tile(i, carry):
        stage_copy(i).wait()
        at = pl.ds(pl.multiple_of(i * tile, tile), tile)
        value = stage[i % 2]
        high = value.astype(jnp.bfloat16)
        a_hi[at, :] = high
        a_lo[at, :] = (value - high.astype(jnp.float32)).astype(jnp.bfloat16)

        @pl.when(i + 2 < tiles)
        def _():
            stage_copy(i + 2).start()

        return carry

    lax.fori_loop(0, tiles, split_tile, 0)

    def multiply(q, block, first, final=False):
        value = gathered[q, block]
        high = value.astype(jnp.bfloat16)
        pieces[:, :width] = high
        pieces[:, width:] = (value - high.astype(jnp.float32)).astype(jnp.bfloat16)
        inner = pl.ds(pl.multiple_of(block * rows, rows), rows)

        def body(i, carry):
            near = (g + 1 + i) % groups
            t = 2 * near + jnp.where(i < groups, 1 - k, k)
            at = pl.ds(pl.multiple_of(t * rows, rows), rows)
            both = jnp.dot(a_hi[at, inner], pieces[...], preferred_element_type=jnp.float32)
            out = jnp.dot(a_lo[at, inner], pieces[:, :width], preferred_element_type=jnp.float32)
            out += both[:, width:]
            out += both[:, :width]
            if first:
                partial[q % 2, t] = out
            else:
                partial[q % 2, t] += out
            if final:
                @pl.when(i < groups)
                def _():
                    pair_copy(q, near).start()

            return carry

        lax.fori_loop(0, cols_axis, body, 0)

    def pair_finish(q):
        for t in range(groups):
            pair_copy(q, t).wait_recv()
        for shift in range(1, groups):
            far = (g + shift) % groups
            partial[q % 2, 2 * far + k] += pair_in[q, far]
            group_copy(q, shift).start()

    def sums_sent(q):
        for t in range(groups):
            pair_copy(q, t).wait_send()
        for shift in range(1, groups):
            group_copy(q, shift).wait_send()

    def total_of(q):
        total = partial[q % 2, c] + pair_in[q, g]
        for shift in range(1, groups):
            group_copy(q, shift).wait_recv()
            total += group_in[q, shift - 1]
        return total

    def store_terms(n, value, j):
        for i in range(rows_axis):
            term[n, j, i] = value[i * height : (i + 1) * height]

    def first_done(_):
        for j in range(cols_axis):
            own_ready(j)
        y_parts = split(-anc_ref[0])
        x_parts = split(wide(own, 0, cols_axis))
        value = dot3(x_parts, y_parts, 0)
        for j in range(cols_axis):
            store_terms(0, value[:, j * span : (j + 1) * span], j)
        each_column(lambda j: term_start(0, j))
        for copy in small:
            copy.wait()
        link_parts = split(link[...])
        value = dot3(y_parts, link_parts, 1)
        for j in range(cols_axis):
            shift_y[j] = value[:, j * width : (j + 1) * width]
        value = dot3(x_parts, link_parts, 1)
        for j in range(cols_axis):
            shift_x[j] = value[:, j * width : (j + 1) * width]
        link_cols = link[pl.ds(pl.multiple_of(c * span, span), span), :]
        value = dot3(split(given[0]), split(link_cols), 1)
        for j in range(cols_axis):
            given_link[j] = value[:, j * span : (j + 1) * span]
        link_terms()

    def own_shifted(j):
        own_ready(cols_axis + j)
        own[cols_axis + j] -= shift_x[j]

    def cross_term(j):
        value = dot3(split(anc_ref[0]), split(own[cols_axis + j]), 0)
        store_terms(1, -value, j)
        term[1, j, r] -= given_link[j]
        term_start(1, j)

    def second_chunk(j, total):
        value = shift_y[j] - total
        anc_ref[1, :, pl.ds(pl.multiple_of(j * width, width), width)] = value

    def link_terms():
        link_rows = link[pl.ds(pl.multiple_of(r * height, height), height), :]
        value = dot3(split(link_rows), split(wide(given_link, 0, cols_axis)), 0)
        for j in range(end):
            store_terms(2, value[:, j * span : (j + 1) * span], j)
        for i in range(end):
            late[i, 1] = value[i * height : (i + 1) * height, end * span :]
        late[end, 1] = jnp.zeros((height, span), jnp.float32)
        for j in range(cols_axis):
            bottom[j] = value[end * height :, j * span : (j + 1) * span]

    def second_terms():
        value = dot3(split(wide(own, cols_axis, end)), split(anc_ref[1, :, : end * width]), 0)
        for j in range(end):
            for i in range(end):
                term[2, j, i] -= value[i * height : (i + 1) * height, j * span : (j + 1) * span]
        each_column(lambda j: term_start(2, j), end)

    def late_terms():
        shifted = split(own[last])
        value = dot3(split(anc_ref[0]), shifted, 0)
        for i in range(rows_axis):
            late[i, 0] = -value[i * height : (i + 1) * height]
        late[r, 0] -= given_link[end]
        done = split(anc_ref[1, :, : end * width])
        value = dot3(done, shifted, 0)
        for i in range(end):
            late[i, 1] -= value[i * height : (i + 1) * height]
        late_start()
        value = dot3(shifted, done, 0)
        for j in range(end):
            bottom[j] -= value[:, j * span : (j + 1) * span]
            bottom_start(j)

    def chunk(q, carry):
        prior = q - 1

        @pl.when(q + 2 <= last)
        def _():
            send_own_block(q + 2)

        @pl.when(q >= 2)
        def _():
            sums_sent(q - 2)

        multiply(q, r, True)

        @pl.when(q >= 1)
        def _():
            pair_finish(prior)

        for i in range(1, rows_axis):
            block = order_of(r, rows_axis, i)
            if i == rows_axis - 1:
                @pl.when(q == cols_axis + 1)
                def _():
                    each_column(lambda j: term_far(0, j))

                @pl.when(q >= cols_axis + 2)
                def _():
                    term_far(1, q - cols_axis - 2)

            if i == rows_axis - 1:
                @pl.when(q == last)
                def _():
                    term_mid(1, end - 1)

            wait_and_forward(q, block)

            @pl.when(r == c)
            def _():
                own_copy(q, block).start()

            multiply(q, block, False, i == rows_axis - 1)
            if i == 1:
                @pl.when(q == cols_axis + 1)
                def _():
                    each_column(lambda j: term_mid(0, j))

                @pl.when(q >= cols_axis + 2)
                def _():
                    term_mid(1, q - cols_axis - 2)

            if i == rows_axis - 1:
                for step in range(rows_axis - 1):
                    @pl.when(q == cols_axis + 1 + step)
                    def _():
                        chain(step)

            if i == 2:
                @pl.when((q >= 1) & (q <= cols_axis))
                def _():
                    at = pl.ds(pl.multiple_of(prior * width, width), width)
                    anc_ref[0, :, at] = -total_of(prior)

                @pl.when(q == cols_axis)
                def _():
                    first_done(None)

                @pl.when(q >= cols_axis + 1)
                def _():
                    j = prior - cols_axis
                    second_chunk(j, total_of(prior))
                    own_shifted(j)
                    cross_term(j)

                @pl.when(q == last)
                def _():
                    second_terms()

        return carry

    lax.fori_loop(0, chunks, chunk, 0)

    @pl.when(c != end - 1)
    def _():
        term_rows(1)

    own_shifted(end)
    late_terms()
    pair_finish(last)
    each_column(lambda j: term_mid(2, j), end)
    term_far(1, end - 1)

    @pl.when(c == end - 1)
    def _():
        term_rows(1)

    late_mid()
    each_column(bottom_mid, end)
    each_column(lambda j: term_far(2, j), end)
    term_rows(2)
    second_chunk(end, total_of(last))
    bottom[end] -= dot3(split(own[last]), split(anc_ref[1, :, end * width :]), 0)
    bottom_start(end)
    late_far()
    each_column(bottom_far, end)
    chain(rows_axis - 1)
    diag_ref[0] = given[0] + term[0, c, r]
    bottom_mid(end)
    bottom_far(end)

    @pl.when(c < end)
    def _():
        cross_ref[...] = term_end(1)

    @pl.when((c < end) & (r < end))
    def _():
        total = term[2, c, r]
        for shift in range(1, rows_axis):
            source = (r + shift) % rows_axis
            tr_wait(2, source).wait_recv()
            total += term_row[2, source]
        diag_ref[1] = given[1] + total

    @pl.when(c == end)
    def _():
        total = late[r]
        for shift in range(1, rows_axis):
            source = (r + shift) % rows_axis
            lr_copy(source, source).wait_recv()
            total += late_row[source]
        cross_ref[...] = total[0]
        diag_ref[1] = given[1] + total[1]

    @pl.when(r == end)
    def _():
        total = given[1] + bottom[c]
        for source in range(end):
            br_copy(source).wait_recv()
            total += bottom_row[source]
        diag_ref[1] = total

    def drain(q, carry):
        def body(block, carry):
            @pl.when((block <= r) & (r + 1 < rows_axis))
            def _():
                hop(q, block, 0, r + 1).wait_send()

            @pl.when((block >= r) & (r >= 1))
            def _():
                hop(q, block, 1, r - 1).wait_send()

            return carry

        lax.fori_loop(0, rows_axis, body, 0)
        for shift in range(1, cols_axis):
            @pl.when(r == c)
            def _():
                own_copy(q, (c + shift) % cols_axis).wait_send()

        return carry

    lax.fori_loop(0, chunks, drain, 0)
    sums_sent(last - 1)
    sums_sent(last)
    each_column(lambda j: term_drain(0, j))
    for n in (1, 2):
        each_column(lambda j: term_drain(n, j), end)
        each_row(n, lambda target: tr_copy(n, target).wait_send())
    chain_drain()
    late_drain()
    each_column(bottom_drain)


def fused(inverse_tile, panels, link_panel, given, tiles):
    rows_axis, cols_axis = lax.axis_size("row"), lax.axis_size("col")
    groups = cols_axis // 2
    full, depth = inverse_tile.shape
    count, rows, columns = panels.shape
    height, span = given.shape[1:]
    width = span
    chunks = count * cols_axis
    tile = min(128, full)
    f32, bf16 = jnp.float32, jnp.bfloat16
    dma = pltpu.SemaphoreType.DMA
    vmem = pltpu.VMEM
    return pl.pallas_call(
        functools.partial(fused_kernel, (rows_axis, cols_axis)),
        out_shape=(
            jax.ShapeDtypeStruct((count, rows, columns), f32),
            jax.ShapeDtypeStruct(given.shape, f32),
            jax.ShapeDtypeStruct((height, span), f32),
        ),
        in_specs=[pl.BlockSpec(memory_space=pltpu.SMEM)] + [pl.BlockSpec(memory_space=pl.ANY)] * 4,
        out_specs=[pl.BlockSpec(memory_space=vmem)] * 3,
        scratch_shapes=[
            vmem((full, depth), bf16),
            vmem((full, depth), bf16),
            vmem((2, tile, depth), f32),
            vmem((rows, 2 * width), bf16),
            vmem((chunks, rows_axis, rows, width), f32),
            vmem((2, cols_axis, rows, width), f32),
            vmem((chunks, groups, rows, width), f32),
            vmem((chunks, max(groups - 1, 1), rows, width), f32),
            vmem((chunks, rows, width), f32),
            vmem((columns, columns), f32),
            vmem(given.shape, f32),
            vmem((cols_axis, rows, width), f32),
            vmem((cols_axis, rows, width), f32),
            vmem((cols_axis, height, span), f32),
            vmem((3, cols_axis, rows_axis, height, span), f32),
            vmem((3, groups, rows_axis, height, span), f32),
            vmem((3, max(groups - 1, 1), rows_axis, height, span), f32),
            vmem((3, rows_axis, height, span), f32),
            dma((2,)),
            dma((chunks,)),
            dma((2,)),
            dma((2, chunks, rows_axis)),
            dma((chunks, rows_axis)),
            dma((chunks, groups)),
            dma((chunks, groups)),
            dma((chunks, max(groups - 1, 1))),
            dma((chunks, max(groups - 1, 1))),
            dma((chunks, cols_axis)),
            dma((chunks,)),
            dma((3, cols_axis)),
            dma((3, cols_axis)),
            dma((3, cols_axis)),
            dma((3, max(groups - 1, 1))),
            dma((3, rows_axis)),
            dma((3, rows_axis)),
            vmem((2, rows_axis, height, span), f32),
            dma((2, rows_axis)),
            dma((2, rows_axis)),
            vmem((rows_axis, 2, height, span), f32),
            vmem((rows_axis, 2, height, span), f32),
            vmem((max(groups - 1, 1), rows_axis, 2, height, span), f32),
            vmem((rows_axis, 2, height, span), f32),
            dma((2,)),
            dma,
            dma((max(groups - 1, 1),)),
            dma((rows_axis,)),
            dma((rows_axis,)),
            vmem((cols_axis, height, span), f32),
            vmem((groups, height, span), f32),
            vmem((max(groups - 1, 1), height, span), f32),
            vmem((rows_axis, height, span), f32),
            dma((cols_axis,)),
            dma((cols_axis,)),
            dma((cols_axis,)),
            dma((max(groups - 1, 1),)),
            dma,
            dma((rows_axis,)),
        ],
        compiler_params=pltpu.CompilerParams(
            collective_id=2, has_side_effects=True, vmem_limit_bytes=58 * 1024 * 1024),
    )(tiles, inverse_tile, panels, link_panel, given)


def local(inverse_tile, panels, link_panel, diag_inverse, ancestor_tiles):
    rows_axis, cols_axis = lax.axis_size("row"), lax.axis_size("col")
    rows, columns = panels.shape[2:]
    square = rows_axis == cols_axis >= 4 and cols_axis % 2 == 0 and rows % TILE == 0 and (columns // cols_axis) % 128 == 0
    if square:
        anc, diag, cross = fused(inverse_tile, panels[0], link_panel[0], diag_inverse[0], ancestor_tiles[0])
    else:
        masked = mask_panels(panels, ancestor_tiles)[0]
        ys, own = products(inverse_tile, masked)
        anc, diag, cross = finish(ys, own, link_panel[0], diag_inverse[0])
    return anc[None], diag[None], cross[None]


def solution(mesh):
    in_specs = (
        P(("hyp", "row"), "col"),
        P("hyp", None, ("col", "row"), None),
        P("hyp", None, None),
        P("hyp", None, "row", "col"),
        P(),
    )
    out_specs = (
        P("hyp", None, ("row", "col"), None),
        P("hyp", None, "row", "col"),
        P("hyp", "row", "col"),
    )
    return jax.shard_map(local, mesh=mesh, in_specs=in_specs, out_specs=out_specs, check_vma=False)
```
